128 devices in a mesh: px: 16 (over y, z_hi, core), py: 8 (over x, z_lo).
Axes of the slice: x: 4, y: 4, z: 4 (z_hi: 2, z_lo: 2; z = z_hi * 2 + z_lo), core: 2. Of those that a mesh axis runs over, the one named last changes fastest.
Arguments:
- level_set: float32 [256, 128, 1024], P('px', 'py'), may hold values from -6 to 6
- flow_amplitude: float32 [3], replicated, may hold values from 0.1 to 0.25
Outputs:
- phi_next: float32 [256, 128, 1024], P('px', 'py')
- vertices: float32 [3, 256, 128, 1024], P(None, 'px', None, 'py')
The draws below stay inside these ranges and needn't reach their ends.
All inputs are finite; a program needn't handle non-finite values.
Results may differ from the reference program's by a relative error of at most 0.0003.
Values sent between devices are 32-bit elements; how exact they have to be, the bound alone decides.
No kernel may reach another device: no remote copies, remote signals or barrier semaphores. Data moves between devices by JAX's collectives and lax.ppermute only.
A program may use at most 64 MiB of HBM per device.

```python
import jax
import jax.numpy as jnp
from jax import lax

CX = 16
NX = 256
NY = 128
NZ = 1024
N_PX = 16


def shard_levels(own_key, dims, shards, low, high):
    factor_of = 1.0
    for position, shards_of in shards:
        heights = jax.random.uniform(jax.random.fold_in(jax.random.fold_in(own_key, 6), position), (shards_of,), jnp.float32, low / len(shards), high / len(shards))
        factor_of = factor_of * jnp.repeat(jnp.exp(heights), dims[position] // shards_of).reshape((-1,) + (1,) * (len(dims) - 1 - position))
    return factor_of


def gaussian(rng, dims, scale, most, split=(), held_as=jnp.bfloat16):
    drawn = jax.random.normal(rng, dims, jnp.float32) * scale
    if len(split) > 0:
        drawn = shard_levels(rng, dims, split, -0.22, 0.18) * drawn
    return jnp.clip(drawn, min=-most, max=most).astype(held_as)


def setup_inputs(seed: int = 0) -> dict:
    seeds = jax.random.split(jax.random.key(seed), 3)
    return {
        "level_set": gaussian(seeds[0], (NX, NY, NZ), 1.0, 6.0, ((0, 16), (1, 8)), jnp.float32),
        "flow_amplitude": jnp.clip(jax.random.uniform(seeds[1], (3,), jnp.float32, 0.1, 0.25), 0.1, 0.25),
    }


weno_eps = 1e-06
sharpness = 4.0
crossing_bias = 0.05
mass_prior = 0.05
tikhonov = 0.25
pseudo_step = 0.5
gradient_eps = 1e-06

def weno_side(delta_one, delta_two, delta_three, delta_four, delta_five):
    guess_one = delta_one / 3.0 - 7.0 * delta_two / 6.0 + 11.0 * delta_three / 6.0
    guess_two = -delta_two / 6.0 + 5.0 * delta_three / 6.0 + delta_four / 3.0
    guess_three = delta_three / 3.0 + 5.0 * delta_four / 6.0 - delta_five / 6.0
    smooth_one = 13.0 / 12.0 * (delta_one - 2.0 * delta_two + delta_three) ** 2 + 0.25 * (delta_one - 4.0 * delta_two + 3.0 * delta_three) ** 2
    smooth_two = 13.0 / 12.0 * (delta_two - 2.0 * delta_three + delta_four) ** 2 + 0.25 * (delta_two - delta_four) ** 2
    smooth_three = 13.0 / 12.0 * (delta_three - 2.0 * delta_four + delta_five) ** 2 + 0.25 * (3.0 * delta_three - 4.0 * delta_four + delta_five) ** 2
    weight_one = 0.1 / (smooth_one + weno_eps) ** 2
    weight_two = 0.6 / (smooth_two + weno_eps) ** 2
    weight_three = 0.3 / (smooth_three + weno_eps) ** 2
    return (weight_one * guess_one + weight_two * guess_two + weight_three * guess_three) / (weight_one + weight_two + weight_three)

def upwind_pair(padded, dimension, length):
    deltas = lax.slice_in_dim(padded, 1, length + 6, axis=dimension) - lax.slice_in_dim(padded, 0, length + 5, axis=dimension)
    window = [lax.slice_in_dim(deltas, offset, offset + length, axis=dimension) for offset in range(6)]
    left_side = weno_side(window[0], window[1], window[2], window[3], window[4])
    right_side = weno_side(window[5], window[4], window[3], window[2], window[1])
    return (left_side, right_side)

def flow_field(flow_amplitude, x_start, y_start, row_count, col_count, layer_count, total_x, total_y, total_z):
    x_cells = ((x_start + jnp.arange(row_count, dtype=jnp.int32)).astype(jnp.float32) + 0.5) / total_x
    y_cells = ((y_start + jnp.arange(col_count, dtype=jnp.int32)).astype(jnp.float32) + 0.5) / total_y
    z_cells = (jnp.arange(layer_count, dtype=jnp.int32).astype(jnp.float32) + 0.5) / total_z
    half_x = jnp.sin(jnp.pi * x_cells) ** 2
    half_y = jnp.sin(jnp.pi * y_cells) ** 2
    half_z = jnp.sin(jnp.pi * z_cells) ** 2
    full_x = jnp.sin(2.0 * jnp.pi * x_cells)
    full_y = jnp.sin(2.0 * jnp.pi * y_cells)
    full_z = jnp.sin(2.0 * jnp.pi * z_cells)
    speed_x = 2.0 * flow_amplitude[0] * half_x[:, None, None] * full_y[None, :, None] * full_z[None, None, :]
    speed_y = -flow_amplitude[1] * full_x[:, None, None] * half_y[None, :, None] * full_z[None, None, :]
    speed_z = -flow_amplitude[2] * full_x[:, None, None] * full_y[None, :, None] * half_z[None, None, :]
    return (speed_x, speed_y, speed_z)

def advect_rate(padded, velocity):
    row_count = padded.shape[0] - 6
    col_count = padded.shape[1] - 6
    centre = padded[3:3 + row_count, 3:3 + col_count, :]
    x_left, x_right = upwind_pair(padded[:, 3:3 + col_count, :], 0, row_count)
    y_left, y_right = upwind_pair(padded[3:3 + row_count, :, :], 1, col_count)
    z_padded = jnp.pad(centre, ((0, 0), (0, 0), (3, 3)), mode='edge')
    z_left, z_right = upwind_pair(z_padded, 2, centre.shape[2])
    speed_x, speed_y, speed_z = velocity
    advection = speed_x * jnp.where(speed_x > 0, x_left, x_right)
    advection = advection + speed_y * jnp.where(speed_y > 0, y_left, y_right)
    advection = advection + speed_z * jnp.where(speed_z > 0, z_left, z_right)
    return -advection

def reinit_sweep(padded):
    centre = padded[1:-1, 1:-1, :]
    smooth_sign = centre / jnp.sqrt(centre * centre + 1.0)
    positive = centre > 0

    def godunov(behind, forward):
        growing = jnp.maximum(jnp.maximum(behind, 0.0) ** 2, jnp.minimum(forward, 0.0) ** 2)
        falling = jnp.maximum(jnp.minimum(behind, 0.0) ** 2, jnp.maximum(forward, 0.0) ** 2)
        return jnp.where(positive, growing, falling)
    x_part = godunov(centre - padded[:-2, 1:-1, :], padded[2:, 1:-1, :] - centre)
    y_part = godunov(centre - padded[1:-1, :-2, :], padded[1:-1, 2:, :] - centre)
    z_padded = jnp.pad(centre, ((0, 0), (0, 0), (1, 1)), mode='edge')
    z_part = godunov(centre - z_padded[:, :, :-2], z_padded[:, :, 2:] - centre)
    magnitude = jnp.sqrt(x_part + y_part + z_part + gradient_eps)
    return centre - pseudo_step * smooth_sign * (magnitude - 1.0)

def set_bit(corner_key, direction, value):
    listed = list(corner_key)
    listed[direction] = value
    return tuple(listed)

def contour(spread, upper_plane):
    row_count = spread.shape[0] - 1
    col_count = spread.shape[1] - 1
    raised_z = jnp.concatenate([spread[:, :, 1:], upper_plane], axis=2)
    corners = {}
    for bit_x in (0, 1):
        for bit_y in (0, 1):
            corners[bit_x, bit_y, 0] = spread[bit_x:bit_x + row_count, bit_y:bit_y + col_count, :]
            corners[bit_x, bit_y, 1] = raised_z[bit_x:bit_x + row_count, bit_y:bit_y + col_count, :]
    ordered = sorted(corners)
    differences = {}
    for direction in range(3):
        for corner_key in ordered:
            if corner_key[direction] == 0:
                differences[direction, corner_key] = corners[set_bit(corner_key, direction, 1)] - corners[corner_key]
    empty_sum = jnp.zeros_like(corners[0, 0, 0])
    weight_sum = empty_sum
    mass_sum = [empty_sum, empty_sum, empty_sum]
    index_pairs = ((0, 0), (0, 1), (0, 2), (1, 1), (1, 2), (2, 2))
    moment = {index_pair: empty_sum for index_pair in index_pairs}
    target = [empty_sum, empty_sum, empty_sum]
    for direction in range(3):
        for corner_key in ordered:
            if corner_key[direction] != 0:
                continue
            value_low = corners[corner_key]
            value_high = corners[set_bit(corner_key, direction, 1)]
            weight = jax.nn.sigmoid(-sharpness * value_low * value_high)
            low_square = value_low * value_low
            fraction = (low_square + crossing_bias) / (low_square + value_high * value_high + 2.0 * crossing_bias)
            normal = [None, None, None]
            normal[direction] = differences[direction, corner_key]
            for across in range(3):
                if across != direction:
                    start_key = set_bit(corner_key, across, 0)
                    end_key = set_bit(start_key, direction, 1)
                    normal[across] = (1.0 - fraction) * differences[across, start_key] + fraction * differences[across, end_key]
            projection = normal[direction] * fraction
            for across in range(3):
                if across != direction and corner_key[across] == 1:
                    projection = projection + normal[across]
            weight_sum = weight_sum + weight
            mass_sum[direction] = mass_sum[direction] + weight * fraction
            for across in range(3):
                if across != direction and corner_key[across] == 1:
                    mass_sum[across] = mass_sum[across] + weight
            for index_pair in index_pairs:
                moment[index_pair] = moment[index_pair] + weight * normal[index_pair[0]] * normal[index_pair[1]]
            weighted = weight * projection
            for across in range(3):
                target[across] = target[across] + weighted * normal[across]
    right_hand = [target[across] + tikhonov * ((mass_sum[across] + 0.5 * mass_prior) / (weight_sum + mass_prior)) for across in range(3)]
    system = {}
    for index_pair in index_pairs:
        system[index_pair] = moment[index_pair] + tikhonov if index_pair[0] == index_pair[1] else moment[index_pair]
    cofactor = {}
    cofactor[0, 0] = system[1, 1] * system[2, 2] - system[1, 2] * system[1, 2]
    cofactor[0, 1] = system[0, 2] * system[1, 2] - system[0, 1] * system[2, 2]
    cofactor[0, 2] = system[0, 1] * system[1, 2] - system[0, 2] * system[1, 1]
    cofactor[1, 1] = system[0, 0] * system[2, 2] - system[0, 2] * system[0, 2]
    cofactor[1, 2] = system[0, 1] * system[0, 2] - system[0, 0] * system[1, 2]
    cofactor[2, 2] = system[0, 0] * system[1, 1] - system[0, 1] * system[0, 1]
    determinant = system[0, 0] * cofactor[0, 0] + system[0, 1] * cofactor[0, 1] + system[0, 2] * cofactor[0, 2]
    solve_x = (cofactor[0, 0] * right_hand[0] + cofactor[0, 1] * right_hand[1] + cofactor[0, 2] * right_hand[2]) / determinant
    solve_y = (cofactor[0, 1] * right_hand[0] + cofactor[1, 1] * right_hand[1] + cofactor[1, 2] * right_hand[2]) / determinant
    solve_z = (cofactor[0, 2] * right_hand[0] + cofactor[1, 2] * right_hand[1] + cofactor[2, 2] * right_hand[2]) / determinant
    return jnp.stack([solve_x, solve_y, solve_z])

def reference(level_set, flow_amplitude):
    starts = jnp.arange(N_PX, dtype=jnp.int32) * CX

    def section_rate(field):
        padded = jnp.pad(field, ((3, 3), (3, 3), (0, 0)), mode='edge')

        def block_rate(start):
            piece = lax.dynamic_slice_in_dim(padded, start, CX + 6, axis=0)
            return advect_rate(piece, flow_field(flow_amplitude, start, 0, CX, NY, NZ, NX, NY, NZ))
        return lax.map(block_rate, starts).reshape(NX, NY, NZ)
    phi_one = level_set + section_rate(level_set)
    phi_two = 0.75 * level_set + 0.25 * (phi_one + section_rate(phi_one))
    phi_three = 1.0 / 3.0 * level_set + 2.0 / 3.0 * (phi_two + section_rate(phi_two))
    padded_three = jnp.pad(phi_three, ((1, 1), (1, 1), (0, 0)), mode='edge')

    def block_sweep(start):
        return reinit_sweep(lax.dynamic_slice_in_dim(padded_three, start, CX + 2, axis=0))
    phi_next = lax.map(block_sweep, starts).reshape(NX, NY, NZ)
    spread = jnp.pad(phi_next, ((0, 1), (0, 1), (0, 0)), mode='edge')

    def block_contour(start):
        piece = lax.dynamic_slice_in_dim(spread, start, CX + 1, axis=0)
        return contour(piece, piece[:, :, NZ - 1:])
    blocks = lax.map(block_contour, starts)
    vertices = jnp.transpose(blocks, (1, 0, 2, 3, 4)).reshape(3, NX, NY, NZ)
    return (phi_next, vertices)
```

```python
import jax
import jax.numpy as jnp
from jax import lax
from jax.experimental import pallas as pl
from jax.experimental.pallas import tpu as pltpu
from jax.sharding import PartitionSpec as P

weno_eps = 1e-06
sharpness = 4.0
crossing_bias = 0.05
mass_prior = 0.05
tikhonov = 0.25
pseudo_step = 0.5
gradient_eps = 1e-06

LOW, HIGH = 10, 11
SHIFT, SLOT = 13, 152
BASE, ROWS, FIRST, SPAN, STEP = 15, 160, 8, 144, 48
VMEM = pl.BlockSpec(memory_space=pltpu.VMEM)
SMEM = pl.BlockSpec(memory_space=pltpu.SMEM)
PARAMS = pltpu.CompilerParams(vmem_limit_bytes=60 * 1024 * 1024)


def pack_kernel(x_ref, out_ref, tall):
    halves, lanes = out_ref.shape[1], out_ref.shape[3]
    layers = x_ref.shape[1]
    for h in range(halves):
        for b in range(layers // lanes):
            tall[h, 16 + b * lanes : 16 + (b + 1) * lanes, :] = x_ref[
                h * lanes : (h + 1) * lanes, b * lanes : (b + 1) * lanes
            ].T
        tall[h, 0:16, :] = jnp.broadcast_to(tall[h, 16:17, :], (16, lanes))
        tall[h, 16 + layers : 32 + layers, :] = jnp.broadcast_to(
            tall[h, 15 + layers : 16 + layers, :], (16, lanes)
        )
    count = out_ref.shape[0]
    for d in range(count):
        start = 16 + d * (layers // count) - SHIFT
        for h in range(halves):
            out_ref[d, h, :, :] = tall[h, start : start + SLOT, :]


def regroup_kernel(in_ref, mid_ref, up_ref, down_ref):
    count, halves, _, lanes = in_ref.shape
    group = lanes // count
    index = lax.broadcasted_iota(jnp.int32, (8, lanes), 1) // group
    rows = mid_ref.shape[0]
    for h in range(halves):

        for t in range(SLOT // 8):
            at = slice(t * 8, t * 8 + 8)
            v = [in_ref[s, h, at, :] for s in range(count)]
            k = count // 2
            while k:
                low_part = (index & k) == 0
                for i in range(count):
                    if i & k:
                        continue
                    a, b = v[i], v[i | k]
                    v[i] = jnp.where(low_part, a, pltpu.roll(b, k * group, 1))
                    v[i | k] = jnp.where(low_part, pltpu.roll(a, lanes - k * group, 1), b)
                k //= 2
            for i in range(count):
                x = h * count + i
                mid_ref[x, at, :] = v[i]
                if x >= rows - LOW:
                    up_ref[x - (rows - LOW), at, :] = v[i]
                if x < HIGH:
                    down_ref[x, at, :] = v[i]


def one_sided(pm2, pm1, p0, pp1, pp2, positive):
    p1 = jnp.where(positive, pm2, pp2)
    p2 = jnp.where(positive, pm1, pp1)
    p4 = jnp.where(positive, pp1, pm1)
    r1 = p2 - p1
    r2 = p0 - p2
    r3 = p4 - p0
    t1 = r2 - r1
    t2 = r3 - r2
    twice_2 = p2 + p2
    y1 = twice_2 + r1
    y2 = twice_2 + r2
    y3 = (p0 + p0) - r3
    k = 13.0 / 3.0
    s1 = (k * r1) * r1 + (y1 * y1 + 4.0 * weno_eps)
    s2 = (k * r2) * r2 + (y2 * y2 + 4.0 * weno_eps)
    s3 = (k * r3) * r3 + (y3 * y3 + 4.0 * weno_eps)
    m1 = s2 * s3
    m2 = s1 * s3
    m3 = s1 * s2
    g1 = m1 * m1
    g2 = (6.0 * m2) * m2
    g3 = (3.0 * m3) * m3
    return r2 + (g1 * (t1 + t1) + g3 * t2) / ((g1 + g3) + g2)


def stage(src, base, dst, coef_refs, scale_ref, lo, count, parts):
    keep, mix = parts
    lanes = src.shape[2]
    lane = lax.broadcasted_iota(jnp.int32, (STEP, lanes), 1)

    def along_lanes(f):
        fp = jnp.where(lane == lanes - 1, f, pltpu.roll(f, lanes - 1, 1))
        fm = jnp.where(lane == 0, f, pltpu.roll(f, 1, 1))
        return (fp - f) - (f - fm), fp - fm

    for start in range(FIRST, FIRST + SPAN, STEP):
        coefs = [ref[start : start + STEP, :] for ref in coef_refs]

        def at(x, shift=0, start=start):
            return src[x, start + shift : start + shift + STEP, :]

        def body(i, carry, start=start, coefs=coefs, at=at):
            x = lo + i
            pm2, pm1, p0, pp1, last, q0, across = carry
            f = at(x)
            following = along_lanes(at(x + 1))
            qm1 = jnp.where(lane < 1, 0.0, pltpu.roll(q0, 1, 1))
            qm2 = jnp.where(lane < 2, 0.0, pltpu.roll(q0, 2, 1))
            qp1 = jnp.where(lane > lanes - 2, 0.0, pltpu.roll(q0, lanes - 1, 1))
            qp2 = jnp.where(lane > lanes - 3, 0.0, pltpu.roll(q0, lanes - 2, 1))
            ahead, near = at(x + 3), at(x + 2)
            step = ahead - near
            pp2 = step - last
            speed = scale_ref[0, x] * coefs[0]
            total = speed * (at(x + 1) - at(x - 1))
            damp = jnp.abs(speed) * one_sided(pm2, pm1, p0, pp1, pp2, speed > 0)
            z = [at(x, shift) for shift in (-3, -2, -1)] + [f]
            z = z + [at(x, shift) for shift in (1, 2, 3)]
            d = [z[n + 1] - z[n] for n in range(6)]
            q = [d[n + 1] - d[n] for n in range(5)]
            speed = scale_ref[2, x] * coefs[2]
            total = total + speed * (z[4] - z[2])
            damp = damp + jnp.abs(speed) * one_sided(*q, speed > 0)
            speed = scale_ref[1, x] * coefs[1]
            total = total + speed * across
            damp = damp + jnp.abs(speed) * one_sided(qm2, qm1, q0, qp1, qp2, speed > 0)
            moved = f - (total - (1.0 / 3.0) * damp)
            if base is not None:
                moved = keep * base[x, start : start + STEP, :] + mix * moved
            dst[x, start : start + STEP, :] = moved
            return (pm1, p0, pp1, pp2, step, *following)

        f = [at(lo + n) for n in range(-3, 3)]
        d = [f[n + 1] - f[n] for n in range(5)]
        p = [d[n + 1] - d[n] for n in range(4)]
        lax.fori_loop(0, count, body, (p[0], p[1], p[2], p[3], d[4], *along_lanes(at(lo))))


def clamp_planes(ref, first, last, lo, hi, begin, end):
    @pl.when(first)
    def _():
        def fill(i, carry):
            ref[lo + i] = ref[begin]
            return carry

        lax.fori_loop(0, begin - lo, fill, 0)

    @pl.when(last)
    def _():
        def fill(i, carry):
            ref[end + i] = ref[end - 1]
            return carry

        lax.fori_loop(0, hi - end, fill, 0)


def clamp_rows(ref, first, last, lo, hi, depth):
    @pl.when(first)
    def _():
        def fill(i, carry):
            x = lo + i
            ref[x, FIRST:BASE, :] = jnp.broadcast_to(
                ref[x, BASE : BASE + 1, :], (BASE - FIRST, ref.shape[2])
            )
            return carry

        lax.fori_loop(0, hi - lo, fill, 0)

    @pl.when(last)
    def _():
        def fill(i, carry):
            x = lo + i
            top = BASE + depth
            ref[x, top : FIRST + SPAN, :] = jnp.broadcast_to(
                ref[x, top - 1 : top, :], (FIRST + SPAN - top, ref.shape[2])
            )
            return carry

        lax.fori_loop(0, hi - lo, fill, 0)


def one_side(positive, behind, forward):
    growing = jnp.maximum(jnp.maximum(behind, 0.0) ** 2, jnp.minimum(forward, 0.0) ** 2)
    falling = jnp.maximum(jnp.minimum(behind, 0.0) ** 2, jnp.maximum(forward, 0.0) ** 2)
    return jnp.where(positive, growing, falling)


def sweep(src, dst, lo, count):
    lanes = src.shape[2]
    lane = lax.broadcasted_iota(jnp.int32, (STEP, lanes), 1)

    def body(i, carry):
        x = lo + i
        for start in range(FIRST, FIRST + SPAN, STEP):

            def at(x, shift=0, start=start):
                return src[x, start + shift : start + shift + STEP, :]

            s = at(x)
            positive = s > 0
            sp = jnp.where(lane == lanes - 1, s, pltpu.roll(s, lanes - 1, 1))
            sm = jnp.where(lane == 0, s, pltpu.roll(s, 1, 1))
            total = one_side(positive, s - at(x - 1), at(x + 1) - s)
            total = total + one_side(positive, s - at(x, -1), at(x, 1) - s)
            total = total + one_side(positive, s - sm, sp - s)
            size = jnp.sqrt(total + gradient_eps)
            sign = s / jnp.sqrt(s * s + 1.0)
            dst[x, start : start + STEP, :] = s - pseudo_step * sign * (size - 1.0)
        return carry

    lax.fori_loop(0, count, body, 0)


def step_kernel(
    place_ref, scale_ref, u_ref, v_ref, w_ref, mid_ref, low_ref, high_ref,
    slots_ref, lower_ref, upper_ref, f0, f1, f2,
):
    own, depth = mid_ref.shape[0], lower_ref.shape[2]
    begin, end = LOW, LOW + own
    first_x = place_ref[0] == 0
    last_x = place_ref[0] == place_ref[2] - 1
    first_z = place_ref[1] == 0
    last_z = place_ref[1] == place_ref[3] - 1
    shift = BASE - SHIFT
    for ref, begin_at in ((low_ref, 0), (mid_ref, begin), (high_ref, end)):

        def move(i, carry, ref=ref, begin_at=begin_at):
            f0[begin_at + i, shift : shift + SLOT, :] = ref[i]
            return carry

        lax.fori_loop(0, ref.shape[0], move, 0)
    clamp_planes(f0, first_x, last_x, 0, end + HIGH, begin, end)
    coefs = (u_ref, v_ref, w_ref)
    plan = ((f0, None, f1, 3, None), (f1, f0, f2, 6, (0.75, 0.25)), (f2, f0, f1, 9, (1.0 / 3.0, 2.0 / 3.0)))
    total = end + HIGH
    for src, base, dst, inset, parts in plan:
        stage(src, base, dst, coefs, scale_ref, inset, total - 2 * inset, parts or (0.0, 1.0))
        clamp_planes(dst, first_x, last_x, inset, total - inset, begin, end)
        clamp_rows(dst, first_z, last_z, inset, total - inset, depth)
    sweep(f1, f0, begin, own + 1)
    clamp_planes(f0, jnp.bool_(False), last_x, begin, end + 1, begin, end)
    clamp_rows(f0, jnp.bool_(False), last_z, begin, end + 1, depth)
    count = slots_ref.shape[0]
    piece = depth // count

    def turn(i, carry):
        lower = f0[begin + i, BASE : BASE + depth, :].T
        upper = f0[begin + i, BASE + 1 : BASE + 1 + depth, :].T
        for ref, value in ((lower_ref, lower), (upper_ref, upper)):
            ref[i, 0:depth, :] = value
            ref[i, depth : depth + 8, :] = jnp.broadcast_to(value[depth - 1 : depth], (8, depth))

        @pl.when(i < own)
        def _():
            for d in range(count):
                slots_ref[d, i] = lower[d * piece : (d + 1) * piece]

        return carry

    lax.fori_loop(0, own + 1, turn, 0)


def edge_terms(a, b):
    weight = 1.0 / (1.0 + jnp.exp2((sharpness * 1.4426950408889634) * (a * b)))
    low = a * a + crossing_bias
    return weight, low / (low + (b * b + crossing_bias))


def contour_kernel(lower_ref, upper_ref, out_ref, wz, tz, wy, ty, wx, tx):
    planes, _, lanes = lower_ref.shape
    depth = lanes
    sides = (lower_ref, upper_ref)

    def edges(x, carry):
        for start in range(0, depth + 8, 8):
            at = slice(start, start + 8)
            wz[x, at, :], tz[x, at, :] = edge_terms(lower_ref[x, at, :], upper_ref[x, at, :])
            for n, ref in enumerate(sides):
                if start < depth:
                    here, there = ref[x, at, :], ref[x, start + 1 : start + 9, :]
                    wy[n, x, at, :], ty[n, x, at, :] = edge_terms(here, there)

                @pl.when(x < planes - 1)
                def _(n=n, ref=ref, at=at, x=x):
                    wx[n, x, at, :], tx[n, x, at, :] = edge_terms(ref[x, at, :], ref[x + 1, at, :])

        return carry

    lax.fori_loop(0, planes, edges, 0)

    def cubes(x, carry):
        for start in range(0, depth, 8):

            def rows(bit, start=start):
                return slice(start + bit, start + bit + 8)

            f = {}
            for bx in (0, 1):
                for by in (0, 1):
                    for bz in (0, 1):
                        f[bx, by, bz] = sides[bz][x + bx, rows(by), :]
            diff = {}
            for d in range(3):
                for key in sorted(f):
                    if key[d] == 0:
                        diff[d, key] = f[set_bit(key, d, 1)] - f[key]
            total = None
            mass = [None] * 3
            moment = {}
            target = [None] * 3

            def add(old, new):
                return new if old is None else old + new

            for d in range(3):
                for key in sorted(f):
                    if key[d] != 0:
                        continue
                    bx, by, bz = key
                    if d == 0:
                        weight, part = wx[bz, x, rows(by), :], tx[bz, x, rows(by), :]
                    elif d == 1:
                        weight, part = wy[bz, x + bx, rows(0), :], ty[bz, x + bx, rows(0), :]
                    else:
                        weight, part = wz[x + bx, rows(by), :], tz[x + bx, rows(by), :]
                    normal = [None] * 3
                    normal[d] = diff[d, key]
                    for a in range(3):
                        if a != d:
                            low = diff[a, set_bit(key, a, 0)]
                            high = diff[a, set_bit(set_bit(key, a, 0), d, 1)]
                            normal[a] = low + part * (high - low)
                    projection = normal[d] * part
                    for a in range(3):
                        if a != d and key[a] == 1:
                            projection = projection + normal[a]
                            mass[a] = add(mass[a], weight)
                    total = add(total, weight)
                    mass[d] = add(mass[d], weight * part)
                    scaled = [weight * n for n in normal]
                    for i in range(3):
                        for j in range(i, 3):
                            moment[i, j] = add(moment.get((i, j)), scaled[i] * normal[j])
                        target[i] = add(target[i], scaled[i] * projection)
            inverse = tikhonov / (total + mass_prior)
            right = [target[i] + (mass[i] + 0.5 * mass_prior) * inverse for i in range(3)]
            for i in range(3):
                moment[i, i] = moment[i, i] + tikhonov
            s = moment
            c00 = s[1, 1] * s[2, 2] - s[1, 2] * s[1, 2]
            c01 = s[0, 2] * s[1, 2] - s[0, 1] * s[2, 2]
            c02 = s[0, 1] * s[1, 2] - s[0, 2] * s[1, 1]
            c11 = s[0, 0] * s[2, 2] - s[0, 2] * s[0, 2]
            c12 = s[0, 1] * s[0, 2] - s[0, 0] * s[1, 2]
            c22 = s[0, 0] * s[1, 1] - s[0, 1] * s[0, 1]
            over = 1.0 / (s[0, 0] * c00 + s[0, 1] * c01 + s[0, 2] * c02)
            out_ref[0, x, rows(0), :] = (c00 * right[0] + c01 * right[1] + c02 * right[2]) * over
            out_ref[1, x, rows(0), :] = (c01 * right[0] + c11 * right[1] + c12 * right[2]) * over
            out_ref[2, x, rows(0), :] = (c02 * right[0] + c12 * right[1] + c22 * right[2]) * over
        return carry

    lax.fori_loop(0, planes - 1, cubes, 0)


def set_bit(key, d, value):
    listed = list(key)
    listed[d] = value
    return tuple(listed)


def speeds(flow_amplitude, x_start, z_start, own, depth, total_x, total_y, total_z):
    def cells(start, count, total):
        return ((start + jnp.arange(count, dtype=jnp.int32)).astype(jnp.float32) + 0.5) / total

    x = cells(x_start - LOW, LOW + own + HIGH, total_x)
    y = cells(0, total_y, total_y)
    z = cells(z_start - BASE, ROWS, total_z)
    half_x, full_x = jnp.sin(jnp.pi * x) ** 2, jnp.sin(2.0 * jnp.pi * x)
    half_y, full_y = jnp.sin(jnp.pi * y) ** 2, jnp.sin(2.0 * jnp.pi * y)
    half_z, full_z = jnp.sin(jnp.pi * z) ** 2, jnp.sin(2.0 * jnp.pi * z)
    scale = jnp.stack(
        [
            flow_amplitude[0] * half_x,
            -0.5 * flow_amplitude[1] * full_x,
            -0.5 * flow_amplitude[2] * full_x,
        ]
    )
    u = full_z[:, None] * full_y[None, :]
    v = full_z[:, None] * half_y[None, :]
    w = half_z[:, None] * full_y[None, :]
    return scale, u, v, w


def shards(level_set, flow_amplitude):
    own, cols, layers = level_set.shape
    count_x, count_z = lax.axis_size("px"), lax.axis_size("py")
    at_x, at_z = lax.axis_index("px"), lax.axis_index("py")
    depth, wide = layers // count_z, cols * count_z
    lanes = 128
    halves = own * cols // lanes
    f32 = jnp.float32
    slots = pl.pallas_call(
        pack_kernel,
        out_shape=jax.ShapeDtypeStruct((count_z, halves, SLOT, lanes), f32),
        in_specs=[VMEM],
        out_specs=VMEM,
        scratch_shapes=[pltpu.VMEM((halves, layers + 32, lanes), f32)],
        compiler_params=PARAMS,
        name="pack",
    )(level_set.reshape(own * cols, layers))
    slots = lax.all_to_all(slots, "py", split_axis=0, concat_axis=0, tiled=True)
    mid, up, down = pl.pallas_call(
        regroup_kernel,
        out_shape=[jax.ShapeDtypeStruct((n, SLOT, wide), f32) for n in (own, LOW, HIGH)],
        in_specs=[VMEM],
        out_specs=[VMEM] * 3,
        compiler_params=PARAMS,
        name="regroup",
    )(slots)
    ring = [(i, (i + 1) % count_x) for i in range(count_x)]
    low = lax.ppermute(up, "px", ring)
    high = lax.ppermute(down, "px", [(b, a) for a, b in ring])
    scale, u, v, w = speeds(
        flow_amplitude, at_x * own, at_z * depth, own, depth, own * count_x, wide, layers
    )
    place = jnp.stack([at_x, at_z, jnp.int32(count_x), jnp.int32(count_z)]).astype(jnp.int32)
    planes = LOW + own + HIGH
    turned, lower, upper = pl.pallas_call(
        step_kernel,
        out_shape=[
            jax.ShapeDtypeStruct((count_z, own, cols, depth), f32),
            jax.ShapeDtypeStruct((own + 1, wide + 8, depth), f32),
            jax.ShapeDtypeStruct((own + 1, wide + 8, depth), f32),
        ],
        in_specs=[SMEM, SMEM] + [VMEM] * 6,
        out_specs=[VMEM] * 3,
        scratch_shapes=[pltpu.VMEM((planes, ROWS, wide), f32)] * 3,
        compiler_params=PARAMS,
        name="advance",
    )(place, scale, u, v, w, mid, low, high)
    back = lax.all_to_all(turned, "py", split_axis=0, concat_axis=0, tiled=True)
    phi_next = jnp.moveaxis(back, 0, 2).reshape(own, cols, layers)
    vertices = pl.pallas_call(
        contour_kernel,
        out_shape=jax.ShapeDtypeStruct((3, own, wide, depth), f32),
        in_specs=[VMEM] * 2,
        out_specs=VMEM,
        scratch_shapes=[pltpu.VMEM((own + 1, wide + 8, depth), f32)] * 2
        + [pltpu.VMEM((2, own + 1, wide, depth), f32)] * 2
        + [pltpu.VMEM((2, own, wide + 8, depth), f32)] * 2,
        compiler_params=PARAMS,
        name="contour",
    )(lower, upper)
    return (phi_next, vertices)


def solution(mesh):
    in_specs = (P("px", "py", None), P())
    out_specs = (P("px", "py", None), P(None, "px", None, "py"))
    return jax.shard_map(shards, mesh=mesh, in_specs=in_specs, out_specs=out_specs, check_vma=False)
```

```python
import jax
import jax.numpy as jnp
from jax import lax
from jax.experimental import pallas as pl
from jax.experimental.pallas import tpu as pltpu
from jax.sharding import PartitionSpec as P

weno_eps = 1e-06
sharpness = 4.0
crossing_bias = 0.05
mass_prior = 0.05
tikhonov = 0.25
pseudo_step = 0.5
gradient_eps = 1e-06

EDGE = 8
LOW, HIGH = 4, 5
SHIFT, SLOT = 13, 152
BASE, ROWS, FIRST, SPAN, STEP = 15, 160, 8, 144, 48
LATE = ((14, 48), (62, 48), (110, 40))
VMEM = pl.BlockSpec(memory_space=pltpu.VMEM)
SMEM = pl.BlockSpec(memory_space=pltpu.SMEM)
PARAMS = pltpu.CompilerParams(vmem_limit_bytes=24 * 1024 * 1024)
WIDE_PARAMS = pltpu.CompilerParams(vmem_limit_bytes=48 * 1024 * 1024)


def pack_kernel(x_ref, out_ref, tall):
    halves, lanes = out_ref.shape[1], out_ref.shape[3]
    layers = x_ref.shape[1]
    for h in range(halves):
        for b in range(layers // lanes):
            tall[h, 16 + b * lanes : 16 + (b + 1) * lanes, :] = x_ref[
                h * lanes : (h + 1) * lanes, b * lanes : (b + 1) * lanes
            ].T
        tall[h, 0:16, :] = jnp.broadcast_to(tall[h, 16:17, :], (16, lanes))
        tall[h, 16 + layers : 32 + layers, :] = jnp.broadcast_to(
            tall[h, 15 + layers : 16 + layers, :], (16, lanes)
        )
    count = out_ref.shape[0]
    for d in range(count):
        start = 16 + d * (layers // count) - SHIFT
        for h in range(halves):
            out_ref[d, h, :, :] = tall[h, start : start + SLOT, :]


def regroup(read, count, lanes, planes, write):
    group = lanes // count
    index = lax.broadcasted_iota(jnp.int32, (8, lanes), 1) // group
    for t in range(SLOT // 8):
        at = slice(t * 8, t * 8 + 8)
        v = [read(n, at) for n in range(count)]
        k = count // 2
        while k:
            low_part = (index & k) == 0
            for i in range(count):
                if i & k:
                    continue
                a, b = v[i], v[i | k]
                v[i] = jnp.where(low_part, a, pltpu.roll(b, k * group, 1))
                v[i | k] = jnp.where(low_part, pltpu.roll(a, lanes - k * group, 1), b)
            k //= 2
        start = BASE - SHIFT + t * 8
        for i in planes:
            write(i, slice(start, start + 8), v[i])


def one_sided(pm2, pm1, p0, pp1, pp2, positive):
    p1 = jnp.where(positive, pm2, pp2)
    p2 = jnp.where(positive, pm1, pp1)
    p4 = jnp.where(positive, pp1, pm1)
    r2 = p0 - p2
    t1 = r2 - (p2 - p1)
    t2 = (p4 - p0) - r2
    k = 39.0 / 64.0
    eps = 0.75 * weno_eps
    c2 = (k * p2) * p2 + eps
    c0 = (k * p0) * p0 + eps
    y1 = p1 - 1.375 * p2
    y2 = p0 - 0.625 * p2
    y3 = p4 - 1.375 * p0
    s1 = y1 * y1 + c2
    s2 = y2 * y2 + c2
    s3 = y3 * y3 + c0
    g1, g2, g3 = [over * over for over in (1.0 / s1, 1.0 / s2, 1.0 / s3)]
    g3 = 3.0 * g3
    return r2 + (g1 * (t1 + t1) + g3 * t2) / ((g1 + g3) + 6.0 * g2)


def stage(src, base, dst, coef_refs, scale_ref, lo, count, parts, rows=None):
    keep, mix = parts
    lanes = src.shape[2]

    def along_lanes(f):
        lane = lax.broadcasted_iota(jnp.int32, f.shape, 1)
        fp = jnp.where(lane == lanes - 1, f, pltpu.roll(f, lanes - 1, 1))
        fm = jnp.where(lane == 0, f, pltpu.roll(f, 1, 1))
        return (fp - f) - (f - fm), fp - fm

    for start, step_rows in rows or [(n, STEP) for n in range(FIRST, FIRST + SPAN, STEP)]:
        part = slice(start, start + step_rows)
        coefs = [ref[part, :] for ref in coef_refs]
        lane = lax.broadcasted_iota(jnp.int32, (step_rows, lanes), 1)

        def at(x, shift=0, start=start, step_rows=step_rows):
            return src[x, start + shift : start + shift + step_rows, :]

        def body(i, carry, part=part, coefs=coefs, lane=lane, at=at):
            x = lo + i
            pm2, pm1, p0, pp1, last, q0, across = carry
            f = at(x)
            following = along_lanes(at(x + 1))
            qm1 = jnp.where(lane < 1, 0.0, pltpu.roll(q0, 1, 1))
            qm2 = jnp.where(lane < 2, 0.0, pltpu.roll(q0, 2, 1))
            qp1 = jnp.where(lane > lanes - 2, 0.0, pltpu.roll(q0, lanes - 1, 1))
            qp2 = jnp.where(lane > lanes - 3, 0.0, pltpu.roll(q0, lanes - 2, 1))
            ahead, near = at(x + 3), at(x + 2)
            step = ahead - near
            pp2 = step - last
            speed = scale_ref[0, x] * coefs[0]
            total = speed * (at(x + 1) - at(x - 1))
            damp = jnp.abs(speed) * one_sided(pm2, pm1, p0, pp1, pp2, speed > 0)
            z = [at(x, shift) for shift in (-3, -2, -1)] + [f]
            z = z + [at(x, shift) for shift in (1, 2, 3)]
            d = [z[n + 1] - z[n] for n in range(6)]
            q = [d[n + 1] - d[n] for n in range(5)]
            speed = scale_ref[2, x] * coefs[2]
            total = total + speed * (z[4] - z[2])
            damp = damp + jnp.abs(speed) * one_sided(*q, speed > 0)
            speed = scale_ref[1, x] * coefs[1]
            total = total + speed * across
            damp = damp + jnp.abs(speed) * one_sided(qm2, qm1, q0, qp1, qp2, speed > 0)
            moved = f - (total - (1.0 / 3.0) * damp)
            if base is not None:
                moved = keep * base[x, part, :] + mix * moved
            dst[x, part, :] = moved
            return (pm1, p0, pp1, pp2, step, *following)

        f = [at(lo + n) for n in range(-3, 3)]
        d = [f[n + 1] - f[n] for n in range(5)]
        p = [d[n + 1] - d[n] for n in range(4)]
        lax.fori_loop(0, count, body, (p[0], p[1], p[2], p[3], d[4], *along_lanes(at(lo))))


def clamp_planes(ref, first, last, lo, hi, begin, end):
    @pl.when(first)
    def _():
        def fill(i, carry):
            ref[lo + i] = ref[begin]
            return carry

        lax.fori_loop(0, begin - lo, fill, 0)

    @pl.when(last)
    def _():
        def fill(i, carry):
            ref[end + i] = ref[end - 1]
            return carry

        lax.fori_loop(0, hi - end, fill, 0)


def clamp_rows(ref, first, last, lo, hi, depth):
    @pl.when(first)
    def _():
        def fill(i, carry):
            x = lo + i
            ref[x, FIRST:BASE, :] = jnp.broadcast_to(
                ref[x, BASE : BASE + 1, :], (BASE - FIRST, ref.shape[2])
            )
            return carry

        lax.fori_loop(0, hi - lo, fill, 0)

    @pl.when(last)
    def _():
        def fill(i, carry):
            x = lo + i
            top = BASE + depth
            ref[x, top : FIRST + SPAN, :] = jnp.broadcast_to(
                ref[x, top - 1 : top, :], (FIRST + SPAN - top, ref.shape[2])
            )
            return carry

        lax.fori_loop(0, hi - lo, fill, 0)


def one_side(positive, behind, forward):
    growing = jnp.maximum(jnp.maximum(behind, 0.0) ** 2, jnp.minimum(forward, 0.0) ** 2)
    falling = jnp.maximum(jnp.minimum(behind, 0.0) ** 2, jnp.maximum(forward, 0.0) ** 2)
    return jnp.where(positive, growing, falling)


def sweep(src, dst, lo, count):
    lanes = src.shape[2]

    def body(i, carry):
        x = lo + i
        for start, step_rows in LATE:
            start = start + 1
            lane = lax.broadcasted_iota(jnp.int32, (step_rows, lanes), 1)

            def at(x, shift=0, start=start, step_rows=step_rows):
                return src[x, start + shift : start + shift + step_rows, :]

            s = at(x)
            positive = s > 0
            sp = jnp.where(lane == lanes - 1, s, pltpu.roll(s, lanes - 1, 1))
            sm = jnp.where(lane == 0, s, pltpu.roll(s, 1, 1))
            total = one_side(positive, s - at(x - 1), at(x + 1) - s)
            total = total + one_side(positive, s - at(x, -1), at(x, 1) - s)
            total = total + one_side(positive, s - sm, sp - s)
            size = jnp.sqrt(total + gradient_eps)
            sign = s / jnp.sqrt(s * s + 1.0)
            dst[x, start : start + step_rows, :] = s - pseudo_step * sign * (size - 1.0)
        return carry

    lax.fori_loop(0, count, body, 0)


def ends(place_ref):
    first_x = place_ref[0] == 0
    last_x = place_ref[0] == place_ref[2] - 1
    first_z = place_ref[1] == 0
    last_z = place_ref[1] == place_ref[3] - 1
    return first_x, last_x, first_z, last_z


def inner_kernel(place_ref, scale_ref, u_ref, v_ref, w_ref, slots_ref, f0, f1):
    count, halves, _, lanes = slots_ref.shape
    own = halves * count
    _, _, first_z, last_z = ends(place_ref)
    for h in range(halves):

        def write(i, rows, value, h=h):
            f0[EDGE + h * count + i, rows, :] = value

        regroup(lambda n, at, h=h: slots_ref[n, h, at, :], count, lanes, range(count), write)
    coefs = (u_ref, v_ref, w_ref)
    stage(f0, None, f1, coefs, scale_ref, EDGE + 3, own - 6, (0.0, 1.0))
    clamp_rows(f1, first_z, last_z, EDGE + 3, EDGE + own - 3, lanes)


def outer_kernel(
    place_ref, scale_ref, u_ref, v_ref, w_ref, below_ref, above_ref, f0_in, f1_in,
    f0, f1, f2, up_ref, down_ref,
):
    del f0_in, f1_in
    count, _, lanes = below_ref.shape
    begin, end = EDGE, f0.shape[0] - EDGE
    first_x, last_x, first_z, last_z = ends(place_ref)
    for ref, at_plane, planes in (
        (below_ref, begin - count, range(count - 6, count)),
        (above_ref, end, range(6)),
    ):

        def write(i, rows, value, at_plane=at_plane):
            f0[at_plane + i, rows, :] = value

        regroup(lambda n, at, ref=ref: ref[n, at, :], count, lanes, planes, write)
    clamp_planes(f0, first_x, last_x, begin - 6, end + 6, begin, end)
    coefs = (u_ref, v_ref, w_ref)
    for lo, hi in ((begin - 3, begin + 3), (end - 3, end + 3)):
        stage(f0, None, f1, coefs, scale_ref, lo, hi - lo, (0.0, 1.0))
    clamp_planes(f1, first_x, last_x, begin - 3, end + 3, begin, end)
    for lo, hi in ((begin - 3, begin + 3), (end - 3, end + 3)):
        clamp_rows(f1, first_z, last_z, lo, hi, lanes)
    for lo, hi in ((begin, begin + HIGH), (end - LOW, end)):
        stage(f1, f0, f2, coefs, scale_ref, lo, hi - lo, (0.75, 0.25))
        clamp_rows(f2, first_z, last_z, lo, hi, lanes)
    for ref, start in ((up_ref, end - LOW), (down_ref, begin)):
        for i in range(ref.shape[0]):
            ref[i] = f2[start + i]


def third_kernel(place_ref, scale_ref, u_ref, v_ref, w_ref, f0, f1, f2_in, f2, f3):
    del f2_in
    _, _, first_z, last_z = ends(place_ref)
    begin, end = EDGE, f0.shape[0] - EDGE
    coefs = (u_ref, v_ref, w_ref)
    lo, hi = begin + HIGH, end - LOW
    stage(f1, f0, f2, coefs, scale_ref, lo, hi - lo, (0.75, 0.25))
    clamp_rows(f2, first_z, last_z, lo, hi, f2.shape[2])
    lo, hi = begin + 3, end - 3
    stage(f2, f0, f3, coefs, scale_ref, lo, hi - lo, (1.0 / 3.0, 2.0 / 3.0), LATE)


def last_kernel(
    place_ref, scale_ref, u_ref, v_ref, w_ref, below_ref, above_ref, f0, f2_in, f3_in,
    f2, f3, slots_ref, lower_ref, upper_ref, f4,
):
    del f2_in, f3_in
    begin, end = EDGE, f0.shape[0] - EDGE
    own, depth = end - begin, lower_ref.shape[2]
    first_x, last_x, first_z, last_z = ends(place_ref)
    for ref, start in ((below_ref, begin - LOW), (above_ref, end)):
        for i in range(ref.shape[0]):
            f2[start + i] = ref[i]
    clamp_planes(f2, first_x, last_x, begin - LOW, end + HIGH, begin, end)
    coefs = (u_ref, v_ref, w_ref)
    for lo, hi in ((begin - 1, begin + 3), (end - 3, end + 2)):
        stage(f2, f0, f3, coefs, scale_ref, lo, hi - lo, (1.0 / 3.0, 2.0 / 3.0), LATE)
    clamp_planes(f3, first_x, last_x, begin - 1, end + 2, begin, end)
    clamp_rows(f3, first_z, last_z, begin - 1, end + 2, depth)
    sweep(f3, f4, begin, own + 1)
    clamp_planes(f4, jnp.bool_(False), last_x, begin, end + 1, begin, end)
    clamp_rows(f4, jnp.bool_(False), last_z, begin, end + 1, depth)
    count = slots_ref.shape[0]
    piece = depth // count

    def turn(i, carry):
        lower = f4[begin + i, BASE : BASE + depth, :].T
        upper = f4[begin + i, BASE + 1 : BASE + 1 + depth, :].T
        for ref, value in ((lower_ref, lower), (upper_ref, upper)):
            ref[i, 0:depth, :] = value
            ref[i, depth : depth + 8, :] = jnp.broadcast_to(value[depth - 1 : depth], (8, depth))

        @pl.when(i < own)
        def _():
            for d in range(count):
                slots_ref[d, i] = lower[d * piece : (d + 1) * piece]

        return carry

    lax.fori_loop(0, own + 1, turn, 0)


def store_edge(refs, at, a, b):
    weight = 1.0 / (1.0 + jnp.exp2((sharpness * 1.4426950408889634) * (a * b)))
    low = a * a + crossing_bias
    part = low / (low + (b * b + crossing_bias))
    along = b - a
    scaled = weight * along
    for ref, value in zip(
        refs, (weight, part, scaled, scaled * along, weight * part, part * along), strict=True
    ):
        ref[at] = value


def add(old, new):
    return new if old is None else old + new


def contour_kernel(lower_ref, upper_ref, out_ref, *scratch):
    planes, _, lanes = lower_ref.shape
    depth = lanes
    sides = (lower_ref, upper_ref)
    x_edges, y_edges, z_edges = scratch[0:6], scratch[6:12], scratch[12:18]

    def across_edges(x, carry):
        for start in range(0, depth + 8, 8):
            at = slice(start, start + 8)
            store_edge(z_edges, (x, at), lower_ref[x, at, :], upper_ref[x, at, :])
            if start < depth:
                for n, ref in enumerate(sides):
                    there = ref[x, start + 1 : start + 9, :]
                    store_edge(y_edges, (n, x, at), ref[x, at, :], there)
        return carry

    lax.fori_loop(0, planes, across_edges, 0)

    def cubes(x, carry):
        for start in range(0, depth + 8, 8):
            at = slice(start, start + 8)
            for n, ref in enumerate(sides):
                store_edge(x_edges, (n, x, at), ref[x, at, :], ref[x + 1, at, :])
        for start in range(0, depth, 8):

            def rows(bit, start=start):
                return slice(start + bit, start + bit + 8)

            f = {}
            for bx in (0, 1):
                for by in (0, 1):
                    for bz in (0, 1):
                        f[bx, by, bz] = sides[bz][x + bx, rows(by), :]
            diff = {}
            for d in range(3):
                for key in sorted(f):
                    if key[d] == 0:
                        diff[d, key] = f[set_bit(key, d, 1)] - f[key]
            total = None
            mass = [None] * 3
            moment = {}
            target = [None] * 3
            twist = {}
            for d in range(3):
                a1, a2 = [a for a in range(3) if a != d]
                weights = {}
                for key in sorted(f):
                    if key[d] != 0:
                        continue
                    bx, by, bz = key
                    refs, at = (
                        (x_edges, (bz, x, rows(by))),
                        (y_edges, (bz, x + bx, rows(0))),
                        (z_edges, (x + bx, rows(by))),
                    )[d]
                    weight, part, scaled_d, square, moved, height = [ref[at] for ref in refs]
                    weights[key[a1], key[a2]] = weight
                    mass[d] = add(mass[d], moved)
                    normal = [None] * 3
                    normal[d] = diff[d, key]
                    scaled = [None] * 3
                    scaled[d] = scaled_d
                    projection = height
                    for a in (a1, a2):
                        low = diff[a, set_bit(key, a, 0)]
                        third = 3 - a - d
                        name = (third, key[third])
                        if name not in twist:
                            twist[name] = diff[a, set_bit(set_bit(key, a, 0), d, 1)] - low
                        normal[a] = low + part * twist[name]
                        scaled[a] = weight * normal[a]
                        if key[a] == 1:
                            projection = projection + normal[a]
                    for i in range(3):
                        for j in range(i, 3):
                            if i == d and j == d:
                                value = square
                            elif j == d:
                                value = scaled[j] * normal[i]
                            else:
                                value = scaled[i] * normal[j]
                            moment[i, j] = add(moment.get((i, j)), value)
                        target[i] = add(target[i], scaled[i] * projection)
                ends = weights[1, 0] + weights[1, 1]
                mass[a1] = add(mass[a1], ends)
                mass[a2] = add(mass[a2], weights[0, 1] + weights[1, 1])
                total = add(total, (weights[0, 0] + weights[0, 1]) + ends)
            inverse = tikhonov / (total + mass_prior)
            r0, r1, r2 = [target[i] + (mass[i] + 0.5 * mass_prior) * inverse for i in range(3)]
            over0 = 1.0 / (moment[0, 0] + tikhonov)
            l1 = moment[0, 1] * over0
            l2 = moment[0, 2] * over0
            over1 = 1.0 / ((moment[1, 1] + tikhonov) - l1 * moment[0, 1])
            rest = moment[1, 2] - l1 * moment[0, 2]
            l3 = rest * over1
            over2 = 1.0 / (((moment[2, 2] + tikhonov) - l2 * moment[0, 2]) - l3 * rest)
            r1 = r1 - l1 * r0
            r2 = (r2 - l2 * r0) - l3 * r1
            x2 = r2 * over2
            x1 = r1 * over1 - l3 * x2
            out_ref[0, x, rows(0), :] = (r0 * over0 - l1 * x1) - l2 * x2
            out_ref[1, x, rows(0), :] = x1
            out_ref[2, x, rows(0), :] = x2
        return carry

    lax.fori_loop(0, planes - 1, cubes, 0)


def set_bit(key, d, value):
    listed = list(key)
    listed[d] = value
    return tuple(listed)


def speeds(flow_amplitude, x_start, z_start, own, depth, total_x, total_y, total_z):
    def cells(start, count, total):
        return ((start + jnp.arange(count, dtype=jnp.int32)).astype(jnp.float32) + 0.5) / total

    x = cells(x_start - EDGE, EDGE + own + EDGE, total_x)
    y = cells(0, total_y, total_y)
    z = cells(z_start - BASE, ROWS, total_z)
    half_x, full_x = jnp.sin(jnp.pi * x) ** 2, jnp.sin(2.0 * jnp.pi * x)
    half_y, full_y = jnp.sin(jnp.pi * y) ** 2, jnp.sin(2.0 * jnp.pi * y)
    half_z, full_z = jnp.sin(jnp.pi * z) ** 2, jnp.sin(2.0 * jnp.pi * z)
    scale = jnp.stack(
        [
            flow_amplitude[0] * half_x,
            -0.5 * flow_amplitude[1] * full_x,
            -0.5 * flow_amplitude[2] * full_x,
        ]
    )
    u = full_z[:, None] * full_y[None, :]
    v = full_z[:, None] * half_y[None, :]
    w = half_z[:, None] * full_y[None, :]
    return scale, u, v, w


def near(value):
    return pltpu.with_memory_space_constraint(value, pltpu.VMEM)


def shards(level_set, flow_amplitude):
    own, cols, layers = level_set.shape
    count_x, count_z = lax.axis_size("px"), lax.axis_size("py")
    at_x, at_z = lax.axis_index("px"), lax.axis_index("py")
    depth, wide = layers // count_z, cols * count_z
    lanes = 128
    halves = own * cols // lanes
    f32 = jnp.float32
    slots = pl.pallas_call(
        pack_kernel,
        out_shape=pltpu.VMEM((count_z, halves, SLOT, lanes), f32),
        in_specs=[VMEM],
        out_specs=VMEM,
        scratch_shapes=[pltpu.VMEM((halves, layers + 32, lanes), f32)],
        compiler_params=PARAMS,
        name="pack",
    )(level_set.reshape(own * cols, layers))
    slots = lax.all_to_all(slots, "py", split_axis=0, concat_axis=0, tiled=True)
    ring = [(i, (i + 1) % count_x) for i in range(count_x)]
    back_ring = [(b, a) for a, b in ring]
    below = lax.ppermute(slots[:, halves - 1], "px", ring)
    above = lax.ppermute(slots[:, 0], "px", back_ring)
    scale, u, v, w = speeds(
        flow_amplitude, at_x * own, at_z * depth, own, depth, own * count_x, wide, layers
    )
    place = jnp.stack([at_x, at_z, jnp.int32(count_x), jnp.int32(count_z)]).astype(jnp.int32)
    planes = EDGE + own + EDGE
    field = pltpu.VMEM((planes, ROWS, wide), f32)
    coefs = [near(a) for a in (u, v, w)]
    f0, f1 = pl.pallas_call(
        inner_kernel,
        out_shape=[field, field],
        in_specs=[SMEM, SMEM] + [VMEM] * 4,
        out_specs=[VMEM] * 2,
        compiler_params=PARAMS,
        name="inner",
    )(place, scale, *coefs, near(slots))
    f0, f1, f2, up, down = pl.pallas_call(
        outer_kernel,
        out_shape=[field, field, field]
        + [pltpu.VMEM((n, ROWS, wide), f32) for n in (LOW, HIGH)],
        in_specs=[SMEM, SMEM] + [VMEM] * 7,
        out_specs=[VMEM] * 5,
        input_output_aliases={7: 0, 8: 1},
        compiler_params=PARAMS,
        name="outer",
    )(place, scale, *coefs, near(below), near(above), near(f0), near(f1))
    below = lax.ppermute(up, "px", ring)
    above = lax.ppermute(down, "px", back_ring)
    f2, f3 = pl.pallas_call(
        third_kernel,
        out_shape=[field, field],
        in_specs=[SMEM, SMEM] + [VMEM] * 6,
        out_specs=[VMEM] * 2,
        input_output_aliases={7: 0},
        compiler_params=PARAMS,
        name="third",
    )(place, scale, *coefs, near(f0), near(f1), near(f2))
    _, _, turned, lower, upper = pl.pallas_call(
        last_kernel,
        out_shape=[
            field,
            field,
            pltpu.VMEM((count_z, own, cols, depth), f32),
            pltpu.VMEM((own + 1, wide + 8, depth), f32),
            pltpu.VMEM((own + 1, wide + 8, depth), f32),
        ],
        in_specs=[SMEM, SMEM] + [VMEM] * 8,
        out_specs=[VMEM] * 5,
        scratch_shapes=[field],
        input_output_aliases={8: 0, 9: 1},
        compiler_params=PARAMS,
        name="last",
    )(place, scale, *coefs, near(below), near(above), near(f0), near(f2), near(f3))
    back = lax.all_to_all(turned, "py", split_axis=0, concat_axis=0, tiled=True)
    phi_next = jnp.moveaxis(back, 0, 2).reshape(own, cols, layers)
    vertices = pl.pallas_call(
        contour_kernel,
        out_shape=jax.ShapeDtypeStruct((3, own, wide, depth), f32),
        in_specs=[VMEM] * 2,
        out_specs=VMEM,
        scratch_shapes=[pltpu.VMEM((2, own, wide + 8, depth), f32)] * 6
        + [pltpu.VMEM((2, own + 1, wide, depth), f32)] * 6
        + [pltpu.VMEM((own + 1, wide + 8, depth), f32)] * 6,
        compiler_params=WIDE_PARAMS,
        name="contour",
    )(near(lower), near(upper))
    return (phi_next, vertices)


def solution(mesh):
    in_specs = (P("px", "py", None), P())
    out_specs = (P("px", "py", None), P(None, "px", None, "py"))
    return jax.shard_map(shards, mesh=mesh, in_specs=in_specs, out_specs=out_specs, check_vma=False)
```

```python
import jax
import jax.numpy as jnp
from jax import lax
from jax.experimental import pallas as pl
from jax.experimental.pallas import tpu as pltpu
from jax.sharding import PartitionSpec as P

weno_eps = 1e-06
sharpness = 4.0
crossing_bias = 0.05
mass_prior = 0.05
tikhonov = 0.25
pseudo_step = 0.5
gradient_eps = 1e-06

EDGE = 8
LOW, HIGH = 4, 5
SHIFT, SLOT = 13, 152
BASE, ROWS, FIRST, SPAN, STEP = 15, 160, 8, 144, 48
PASS = 32
LATE = ((14, 48), (62, 48), (110, 40))
VMEM = pl.BlockSpec(memory_space=pltpu.VMEM)
SMEM = pl.BlockSpec(memory_space=pltpu.SMEM)
PARAMS = pltpu.CompilerParams(vmem_limit_bytes=24 * 1024 * 1024)
WIDE_PARAMS = pltpu.CompilerParams(vmem_limit_bytes=26 * 1024 * 1024)


def pack_kernel(x_ref, out_ref, tall):
    halves, lanes = out_ref.shape[1], out_ref.shape[3]
    layers = x_ref.shape[1]
    for h in range(halves):
        for b in range(layers // lanes):
            tall[h, 16 + b * lanes : 16 + (b + 1) * lanes, :] = x_ref[
                h * lanes : (h + 1) * lanes, b * lanes : (b + 1) * lanes
            ].T
        tall[h, 0:16, :] = jnp.broadcast_to(tall[h, 16:17, :], (16, lanes))
        tall[h, 16 + layers : 32 + layers, :] = jnp.broadcast_to(
            tall[h, 15 + layers : 16 + layers, :], (16, lanes)
        )
    count = out_ref.shape[0]
    for d in range(count):
        start = 16 + d * (layers // count) - SHIFT
        for h in range(halves):
            out_ref[d, h, :, :] = tall[h, start : start + SLOT, :]


def regroup(read, count, lanes, planes, write):
    group = lanes // count
    for first in range(0, SLOT, PASS):
        rows = min(PASS, SLOT - first)
        index = lax.broadcasted_iota(jnp.int32, (rows, lanes), 1) // group
        v = [read(n, slice(first, first + rows)) for n in range(count)]
        k = count // 2
        while k:
            low_part = (index & k) == 0
            pairs = [(i, i | k) for i in range(count) if not i & k]
            moved = [
                (pltpu.roll(v[j], k * group, 1), pltpu.roll(v[i], lanes - k * group, 1))
                for i, j in pairs
            ]
            for (i, j), (from_j, from_i) in zip(pairs, moved, strict=True):
                v[i] = jnp.where(low_part, v[i], from_j)
                v[j] = jnp.where(low_part, from_i, v[j])
            k //= 2
        start = BASE - SHIFT + first
        for i in planes:
            write(i, slice(start, start + rows), v[i])


def one_sided(pm2, pm1, p0, pp1, pp2, positive):
    p1 = jnp.where(positive, pm2, pp2)
    p2 = jnp.where(positive, pm1, pp1)
    p4 = jnp.where(positive, pp1, pm1)
    r2 = p0 - p2
    t1 = r2 - (p2 - p1)
    t2 = (p4 - p0) - r2
    k = 39.0 / 64.0
    eps = 0.75 * weno_eps
    c2 = (k * p2) * p2 + eps
    c0 = (k * p0) * p0 + eps
    y1 = p1 - 1.375 * p2
    y2 = p0 - 0.625 * p2
    y3 = p4 - 1.375 * p0
    s1 = y1 * y1 + c2
    s2 = y2 * y2 + c2
    s3 = y3 * y3 + c0
    g1, g2, g3 = [over * over for over in (1.0 / s1, 1.0 / s2, 1.0 / s3)]
    g3 = 3.0 * g3
    return r2 + (g1 * (t1 + t1) + g3 * t2) / ((g1 + g3) + 6.0 * g2)


def stage(src, base, dst, coef_refs, scale_ref, lo, count, parts, rows=None):
    keep, mix = parts
    lanes = src.shape[2]

    def along_lanes(f):
        lane = lax.broadcasted_iota(jnp.int32, f.shape, 1)
        fp = jnp.where(lane == lanes - 1, f, pltpu.roll(f, lanes - 1, 1))
        fm = jnp.where(lane == 0, f, pltpu.roll(f, 1, 1))
        return (fp - f) - (f - fm), fp - fm

    for start, step_rows in rows or [(n, STEP) for n in range(FIRST, FIRST + SPAN, STEP)]:
        part = slice(start, start + step_rows)
        coefs = [ref[part, :] for ref in coef_refs]
        lane = lax.broadcasted_iota(jnp.int32, (step_rows, lanes), 1)

        def at(x, shift=0, start=start, step_rows=step_rows):
            return src[x, start + shift : start + shift + step_rows, :]

        def body(i, carry, part=part, coefs=coefs, lane=lane, at=at):
            x = lo + i
            pm2, pm1, p0, pp1, last, q0, across = carry
            f = at(x)
            following = along_lanes(at(x + 1))
            qm1 = jnp.where(lane < 1, 0.0, pltpu.roll(q0, 1, 1))
            qm2 = jnp.where(lane < 2, 0.0, pltpu.roll(q0, 2, 1))
            qp1 = jnp.where(lane > lanes - 2, 0.0, pltpu.roll(q0, lanes - 1, 1))
            qp2 = jnp.where(lane > lanes - 3, 0.0, pltpu.roll(q0, lanes - 2, 1))
            ahead, near = at(x + 3), at(x + 2)
            step = ahead - near
            pp2 = step - last
            speed = scale_ref[0, x] * coefs[0]
            total = speed * (at(x + 1) - at(x - 1))
            damp = jnp.abs(speed) * one_sided(pm2, pm1, p0, pp1, pp2, speed > 0)
            z = [at(x, shift) for shift in (-3, -2, -1)] + [f]
            z = z + [at(x, shift) for shift in (1, 2, 3)]
            d = [z[n + 1] - z[n] for n in range(6)]
            q = [d[n + 1] - d[n] for n in range(5)]
            speed = scale_ref[2, x] * coefs[2]
            total = total + speed * (z[4] - z[2])
            damp = damp + jnp.abs(speed) * one_sided(*q, speed > 0)
            speed = scale_ref[1, x] * coefs[1]
            total = total + speed * across
            damp = damp + jnp.abs(speed) * one_sided(qm2, qm1, q0, qp1, qp2, speed > 0)
            moved = f - (total - (1.0 / 3.0) * damp)
            if base is not None:
                moved = keep * base[x, part, :] + mix * moved
            dst[x, part, :] = moved
            return (pm1, p0, pp1, pp2, step, *following)

        f = [at(lo + n) for n in range(-3, 3)]
        d = [f[n + 1] - f[n] for n in range(5)]
        p = [d[n + 1] - d[n] for n in range(4)]
        lax.fori_loop(0, count, body, (p[0], p[1], p[2], p[3], d[4], *along_lanes(at(lo))))


def clamp_planes(ref, first, last, lo, hi, begin, end):
    @pl.when(first)
    def _():
        def fill(i, carry):
            ref[lo + i] = ref[begin]
            return carry

        lax.fori_loop(0, begin - lo, fill, 0)

    @pl.when(last)
    def _():
        def fill(i, carry):
            ref[end + i] = ref[end - 1]
            return carry

        lax.fori_loop(0, hi - end, fill, 0)


def clamp_rows(ref, first, last, lo, hi, depth):
    @pl.when(first)
    def _():
        def fill(i, carry):
            x = lo + i
            ref[x, FIRST:BASE, :] = jnp.broadcast_to(
                ref[x, BASE : BASE + 1, :], (BASE - FIRST, ref.shape[2])
            )
            return carry

        lax.fori_loop(0, hi - lo, fill, 0)

    @pl.when(last)
    def _():
        def fill(i, carry):
            x = lo + i
            top = BASE + depth
            ref[x, top : FIRST + SPAN, :] = jnp.broadcast_to(
                ref[x, top - 1 : top, :], (FIRST + SPAN - top, ref.shape[2])
            )
            return carry

        lax.fori_loop(0, hi - lo, fill, 0)


def one_side(positive, s, behind, ahead):
    drop = s - jnp.minimum(behind, ahead)
    rise = jnp.maximum(behind, ahead) - s
    steep = jnp.maximum(jnp.where(positive, drop, rise), 0.0)
    return steep * steep


def sweep(src, dst, lo, count):
    lanes = src.shape[2]

    def body(i, carry):
        x = lo + i
        for start, step_rows in LATE:
            start = start + 1
            lane = lax.broadcasted_iota(jnp.int32, (step_rows, lanes), 1)

            def at(x, shift=0, start=start, step_rows=step_rows):
                return src[x, start + shift : start + shift + step_rows, :]

            s = at(x)
            positive = s > 0
            sp = jnp.where(lane == lanes - 1, s, pltpu.roll(s, lanes - 1, 1))
            sm = jnp.where(lane == 0, s, pltpu.roll(s, 1, 1))
            total = one_side(positive, s, at(x - 1), at(x + 1))
            total = total + one_side(positive, s, at(x, -1), at(x, 1))
            total = total + one_side(positive, s, sm, sp)
            total = total + gradient_eps
            size = total * lax.rsqrt(total)
            sign = s * lax.rsqrt(s * s + 1.0)
            dst[x, start : start + step_rows, :] = s - pseudo_step * sign * (size - 1.0)
        return carry

    lax.fori_loop(0, count, body, 0)


def ends(place_ref):
    first_x = place_ref[0] == 0
    last_x = place_ref[0] == place_ref[2] - 1
    first_z = place_ref[1] == 0
    last_z = place_ref[1] == place_ref[3] - 1
    return first_x, last_x, first_z, last_z


def inner_kernel(place_ref, scale_ref, u_ref, v_ref, w_ref, slots_ref, f0, f1):
    count, halves, _, lanes = slots_ref.shape
    own = halves * count
    _, _, first_z, last_z = ends(place_ref)
    for h in range(halves):

        def write(i, rows, value, h=h):
            f0[EDGE + h * count + i, rows, :] = value

        regroup(lambda n, at, h=h: slots_ref[n, h, at, :], count, lanes, range(count), write)
    coefs = (u_ref, v_ref, w_ref)
    stage(f0, None, f1, coefs, scale_ref, EDGE + 3, own - 6, (0.0, 1.0))
    clamp_rows(f1, first_z, last_z, EDGE + 3, EDGE + own - 3, lanes)


def outer_kernel(
    place_ref, scale_ref, u_ref, v_ref, w_ref, below_ref, above_ref, f0_in, f1_in,
    f0, f1, f2, up_ref, down_ref,
):
    del f0_in, f1_in
    count, _, lanes = below_ref.shape
    begin, end = EDGE, f0.shape[0] - EDGE
    first_x, last_x, first_z, last_z = ends(place_ref)
    for ref, at_plane, planes in (
        (below_ref, begin - count, range(count - 6, count)),
        (above_ref, end, range(6)),
    ):

        def write(i, rows, value, at_plane=at_plane):
            f0[at_plane + i, rows, :] = value

        regroup(lambda n, at, ref=ref: ref[n, at, :], count, lanes, planes, write)
    clamp_planes(f0, first_x, last_x, begin - 6, end + 6, begin, end)
    coefs = (u_ref, v_ref, w_ref)
    for lo, hi in ((begin - 3, begin + 3), (end - 3, end + 3)):
        stage(f0, None, f1, coefs, scale_ref, lo, hi - lo, (0.0, 1.0))
    clamp_planes(f1, first_x, last_x, begin - 3, end + 3, begin, end)
    for lo, hi in ((begin - 3, begin + 3), (end - 3, end + 3)):
        clamp_rows(f1, first_z, last_z, lo, hi, lanes)
    for lo, hi in ((begin, begin + HIGH), (end - LOW, end)):
        stage(f1, f0, f2, coefs, scale_ref, lo, hi - lo, (0.75, 0.25))
        clamp_rows(f2, first_z, last_z, lo, hi, lanes)
    for ref, start in ((up_ref, end - LOW), (down_ref, begin)):
        for i in range(ref.shape[0]):
            ref[i] = f2[start + i]


def third_kernel(place_ref, scale_ref, u_ref, v_ref, w_ref, f0, f1, f2_in, f2, f3):
    del f2_in
    _, _, first_z, last_z = ends(place_ref)
    begin, end = EDGE, f0.shape[0] - EDGE
    coefs = (u_ref, v_ref, w_ref)
    lo, hi = begin + HIGH, end - LOW
    stage(f1, f0, f2, coefs, scale_ref, lo, hi - lo, (0.75, 0.25))
    clamp_rows(f2, first_z, last_z, lo, hi, f2.shape[2])
    lo, hi = begin + 3, end - 3
    stage(f2, f0, f3, coefs, scale_ref, lo, hi - lo, (1.0 / 3.0, 2.0 / 3.0), LATE)


def last_kernel(
    place_ref, scale_ref, u_ref, v_ref, w_ref, below_ref, above_ref, f0, f2_in, f3_in,
    f2, f3, slots_ref, lower_ref, upper_ref, f4,
):
    del f2_in, f3_in
    begin, end = EDGE, f0.shape[0] - EDGE
    own, depth = end - begin, lower_ref.shape[2]
    first_x, last_x, first_z, last_z = ends(place_ref)
    for ref, start in ((below_ref, begin - LOW), (above_ref, end)):
        for i in range(ref.shape[0]):
            f2[start + i] = ref[i]
    clamp_planes(f2, first_x, last_x, begin - LOW, end + HIGH, begin, end)
    coefs = (u_ref, v_ref, w_ref)
    for lo, hi in ((begin - 1, begin + 3), (end - 3, end + 2)):
        stage(f2, f0, f3, coefs, scale_ref, lo, hi - lo, (1.0 / 3.0, 2.0 / 3.0), LATE)
    clamp_planes(f3, first_x, last_x, begin - 1, end + 2, begin, end)
    clamp_rows(f3, first_z, last_z, begin - 1, end + 2, depth)
    sweep(f3, f4, begin, own + 1)
    clamp_planes(f4, jnp.bool_(False), last_x, begin, end + 1, begin, end)
    clamp_rows(f4, jnp.bool_(False), last_z, begin, end + 1, depth)
    count = slots_ref.shape[0]
    piece = depth // count

    def turn(i, carry):
        lower = f4[begin + i, BASE : BASE + depth, :].T
        upper = f4[begin + i, BASE + 1 : BASE + 1 + depth, :].T
        for ref, value in ((lower_ref, lower), (upper_ref, upper)):
            ref[i, 0:depth, :] = value
            ref[i, depth : depth + 8, :] = jnp.broadcast_to(value[depth - 1 : depth], (8, depth))

        @pl.when(i < own)
        def _():
            for d in range(count):
                slots_ref[d, i] = lower[d * piece : (d + 1) * piece]

        return carry

    lax.fori_loop(0, own + 1, turn, 0)


def store_edge(refs, at, a, b):
    weight = 1.0 / (1.0 + jnp.exp2((sharpness * 1.4426950408889634) * (a * b)))
    low = a * a + crossing_bias
    part = low / (low + (b * b + crossing_bias))
    along = b - a
    scaled = weight * along
    for ref, value in zip(
        refs, (weight, part, scaled, scaled * along, weight * part, part * along), strict=True
    ):
        ref[at] = value


def add(old, new):
    return new if old is None else old + new


def contour_kernel(lower_ref, upper_ref, out_ref, *scratch):
    planes, _, lanes = lower_ref.shape
    depth = lanes
    sides = (lower_ref, upper_ref)
    x_edges, y_edges, z_edges = scratch[0:6], scratch[6:12], scratch[12:18]

    def across_edges(x, carry):
        for start in range(0, depth + 8, 8):
            at = slice(start, start + 8)
            store_edge(z_edges, (x, at), lower_ref[x, at, :], upper_ref[x, at, :])
            if start < depth:
                for n, ref in enumerate(sides):
                    there = ref[x, start + 1 : start + 9, :]
                    store_edge(y_edges, (n, x, at), ref[x, at, :], there)
        return carry

    @pl.when(pl.program_id(0) == 0)
    def _():
        lax.fori_loop(0, planes, across_edges, 0)

    def cubes(x):
        for start in range(0, depth + 8, 8):
            at = slice(start, start + 8)
            for n, ref in enumerate(sides):
                store_edge(x_edges, (n, at), ref[x, at, :], ref[x + 1, at, :])
        for start in range(0, depth, 8):

            def rows(bit, start=start):
                return slice(start + bit, start + bit + 8)

            f = {}
            for bx in (0, 1):
                for by in (0, 1):
                    for bz in (0, 1):
                        f[bx, by, bz] = sides[bz][x + bx, rows(by), :]
            diff = {}
            for d in range(3):
                for key in sorted(f):
                    if key[d] == 0:
                        diff[d, key] = f[set_bit(key, d, 1)] - f[key]
            total = None
            mass = [None] * 3
            moment = {}
            target = [None] * 3
            twist = {}
            for d in range(3):
                a1, a2 = [a for a in range(3) if a != d]
                weights = {}
                for key in sorted(f):
                    if key[d] != 0:
                        continue
                    bx, by, bz = key
                    refs, at = (
                        (x_edges, (bz, rows(by))),
                        (y_edges, (bz, x + bx, rows(0))),
                        (z_edges, (x + bx, rows(by))),
                    )[d]
                    weight, part, scaled_d, square, moved, height = [ref[at] for ref in refs]
                    weights[key[a1], key[a2]] = weight
                    mass[d] = add(mass[d], moved)
                    normal = [None] * 3
                    normal[d] = diff[d, key]
                    scaled = [None] * 3
                    scaled[d] = scaled_d
                    projection = height
                    for a in (a1, a2):
                        low = diff[a, set_bit(key, a, 0)]
                        third = 3 - a - d
                        name = (third, key[third])
                        if name not in twist:
                            twist[name] = diff[a, set_bit(set_bit(key, a, 0), d, 1)] - low
                        normal[a] = low + part * twist[name]
                        scaled[a] = weight * normal[a]
                        if key[a] == 1:
                            projection = projection + normal[a]
                    for i in range(3):
                        for j in range(i, 3):
                            if i == d and j == d:
                                value = square
                            elif j == d:
                                value = scaled[j] * normal[i]
                            else:
                                value = scaled[i] * normal[j]
                            moment[i, j] = add(moment.get((i, j)), value)
                        target[i] = add(target[i], scaled[i] * projection)
                ends = weights[1, 0] + weights[1, 1]
                mass[a1] = add(mass[a1], ends)
                mass[a2] = add(mass[a2], weights[0, 1] + weights[1, 1])
                total = add(total, (weights[0, 0] + weights[0, 1]) + ends)
            inverse = tikhonov / (total + mass_prior)
            r0, r1, r2 = [target[i] + (mass[i] + 0.5 * mass_prior) * inverse for i in range(3)]
            over0 = 1.0 / (moment[0, 0] + tikhonov)
            l1 = moment[0, 1] * over0
            l2 = moment[0, 2] * over0
            over1 = 1.0 / ((moment[1, 1] + tikhonov) - l1 * moment[0, 1])
            rest = moment[1, 2] - l1 * moment[0, 2]
            l3 = rest * over1
            over2 = 1.0 / (((moment[2, 2] + tikhonov) - l2 * moment[0, 2]) - l3 * rest)
            r1 = r1 - l1 * r0
            r2 = (r2 - l2 * r0) - l3 * r1
            x2 = r2 * over2
            x1 = r1 * over1 - l3 * x2
            out_ref[0, 0, rows(0), :] = (r0 * over0 - l1 * x1) - l2 * x2
            out_ref[1, 0, rows(0), :] = x1
            out_ref[2, 0, rows(0), :] = x2

    cubes(pl.program_id(0))


def set_bit(key, d, value):
    listed = list(key)
    listed[d] = value
    return tuple(listed)


def speeds(flow_amplitude, x_start, z_start, own, depth, total_x, total_y, total_z):
    def cells(start, count, total):
        return ((start + jnp.arange(count, dtype=jnp.int32)).astype(jnp.float32) + 0.5) / total

    x = cells(x_start - EDGE, EDGE + own + EDGE, total_x)
    y = cells(0, total_y, total_y)
    z = cells(z_start - BASE, ROWS, total_z)
    half_x, full_x = jnp.sin(jnp.pi * x) ** 2, jnp.sin(2.0 * jnp.pi * x)
    half_y, full_y = jnp.sin(jnp.pi * y) ** 2, jnp.sin(2.0 * jnp.pi * y)
    half_z, full_z = jnp.sin(jnp.pi * z) ** 2, jnp.sin(2.0 * jnp.pi * z)
    scale = jnp.stack(
        [
            flow_amplitude[0] * half_x,
            -0.5 * flow_amplitude[1] * full_x,
            -0.5 * flow_amplitude[2] * full_x,
        ]
    )
    u = full_z[:, None] * full_y[None, :]
    v = full_z[:, None] * half_y[None, :]
    w = half_z[:, None] * full_y[None, :]
    return scale, u, v, w


def near(value):
    return pltpu.with_memory_space_constraint(value, pltpu.VMEM)


def shards(level_set, flow_amplitude):
    own, cols, layers = level_set.shape
    count_x, count_z = lax.axis_size("px"), lax.axis_size("py")
    at_x, at_z = lax.axis_index("px"), lax.axis_index("py")
    depth, wide = layers // count_z, cols * count_z
    lanes = 128
    halves = own * cols // lanes
    f32 = jnp.float32
    slots = pl.pallas_call(
        pack_kernel,
        out_shape=pltpu.VMEM((count_z, halves, SLOT, lanes), f32),
        in_specs=[VMEM],
        out_specs=VMEM,
        scratch_shapes=[pltpu.VMEM((halves, layers + 32, lanes), f32)],
        compiler_params=PARAMS,
        name="pack",
    )(level_set.reshape(own * cols, layers))
    slots = lax.all_to_all(slots, "py", split_axis=0, concat_axis=0, tiled=True)
    scale, u, v, w = speeds(
        flow_amplitude, at_x * own, at_z * depth, own, depth, own * count_x, wide, layers
    )
    place = jnp.stack([at_x, at_z, jnp.int32(count_x), jnp.int32(count_z)]).astype(jnp.int32)
    ring = [(i, (i + 1) % count_x) for i in range(count_x)]
    back_ring = [(b, a) for a, b in ring]
    below = lax.ppermute(slots[:, halves - 1], "px", ring)
    above = lax.ppermute(slots[:, 0], "px", back_ring)
    planes = EDGE + own + EDGE
    field = pltpu.VMEM((planes, ROWS, wide), f32)
    coefs = [near(a) for a in (u, v, w)]
    f0, f1 = pl.pallas_call(
        inner_kernel,
        out_shape=[field, field],
        in_specs=[SMEM, SMEM] + [VMEM] * 4,
        out_specs=[VMEM] * 2,
        compiler_params=PARAMS,
        name="inner",
    )(place, scale, *coefs, near(slots))
    f0, f1, f2, up, down = pl.pallas_call(
        outer_kernel,
        out_shape=[field, field, field]
        + [pltpu.VMEM((n, ROWS, wide), f32) for n in (LOW, HIGH)],
        in_specs=[SMEM, SMEM] + [VMEM] * 7,
        out_specs=[VMEM] * 5,
        input_output_aliases={7: 0, 8: 1},
        compiler_params=PARAMS,
        name="outer",
    )(place, scale, *coefs, near(below), near(above), near(f0), near(f1))
    below = lax.ppermute(up, "px", ring)
    above = lax.ppermute(down, "px", back_ring)
    f2, f3 = pl.pallas_call(
        third_kernel,
        out_shape=[field, field],
        in_specs=[SMEM, SMEM] + [VMEM] * 6,
        out_specs=[VMEM] * 2,
        input_output_aliases={7: 0},
        compiler_params=PARAMS,
        name="third",
    )(place, scale, *coefs, near(f0), near(f1), near(f2))
    _, _, turned, lower, upper = pl.pallas_call(
        last_kernel,
        out_shape=[
            field,
            field,
            pltpu.VMEM((count_z, own, cols, depth), f32),
            pltpu.VMEM((own + 1, wide + 8, depth), f32),
            pltpu.VMEM((own + 1, wide + 8, depth), f32),
        ],
        in_specs=[SMEM, SMEM] + [VMEM] * 8,
        out_specs=[VMEM] * 5,
        scratch_shapes=[field],
        input_output_aliases={8: 0, 9: 1},
        compiler_params=PARAMS,
        name="last",
    )(place, scale, *coefs, near(below), near(above), near(f0), near(f2), near(f3))
    back = lax.all_to_all(turned, "py", split_axis=0, concat_axis=0, tiled=True)
    phi_next = jnp.moveaxis(back, 0, 2).reshape(own, cols, layers)
    vertices = pl.pallas_call(
        contour_kernel,
        out_shape=jax.ShapeDtypeStruct((3, own, wide, depth), f32),
        grid=(own,),
        in_specs=[VMEM] * 2,
        out_specs=pl.BlockSpec((3, 1, wide, depth), lambda i: (0, i, 0, 0)),
        scratch_shapes=[pltpu.VMEM((2, wide + 8, depth), f32)] * 6
        + [pltpu.VMEM((2, own + 1, wide, depth), f32)] * 6
        + [pltpu.VMEM((own + 1, wide + 8, depth), f32)] * 6,
        compiler_params=WIDE_PARAMS,
        name="contour",
    )(near(lower), near(upper))
    return (phi_next, vertices)


def solution(mesh):
    in_specs = (P("px", "py", None), P())
    out_specs = (P("px", "py", None), P(None, "px", None, "py"))
    return jax.shard_map(shards, mesh=mesh, in_specs=in_specs, out_specs=out_specs, check_vma=False)
```

```python
import jax
import jax.numpy as jnp
from jax import lax
from jax.experimental import pallas as pl
from jax.experimental.pallas import tpu as pltpu
from jax.sharding import PartitionSpec as P

weno_eps = 1e-06
sharpness = 4.0
crossing_bias = 0.05
mass_prior = 0.05
tikhonov = 0.25
pseudo_step = 0.5
gradient_eps = 1e-06

EDGE = 8
LOW, HIGH = 4, 5
SHIFT, SLOT = 13, 152
BASE, ROWS, FIRST, SPAN, STEP = 15, 160, 8, 144, 48
PASS = 32
LATE = ((14, 48), (62, 48), (110, 40))
VMEM = pl.BlockSpec(memory_space=pltpu.VMEM)
SMEM = pl.BlockSpec(memory_space=pltpu.SMEM)
PARAMS = pltpu.CompilerParams(vmem_limit_bytes=24 * 1024 * 1024)
WIDE_PARAMS = pltpu.CompilerParams(vmem_limit_bytes=26 * 1024 * 1024)


def pack_kernel(x_ref, out_ref, tall):
    halves, lanes = out_ref.shape[1], out_ref.shape[3]
    layers = x_ref.shape[1]
    for h in range(halves):
        for b in range(layers // lanes):
            tall[h, 16 + b * lanes : 16 + (b + 1) * lanes, :] = x_ref[
                h * lanes : (h + 1) * lanes, b * lanes : (b + 1) * lanes
            ].T
        tall[h, 0:16, :] = jnp.broadcast_to(tall[h, 16:17, :], (16, lanes))
        tall[h, 16 + layers : 32 + layers, :] = jnp.broadcast_to(
            tall[h, 15 + layers : 16 + layers, :], (16, lanes)
        )
    count = out_ref.shape[0]
    for d in range(count):
        start = 16 + d * (layers // count) - SHIFT
        for h in range(halves):
            out_ref[d, h, :, :] = tall[h, start : start + SLOT, :]


def regroup(read, count, lanes, planes, write):
    group = lanes // count
    for first in range(0, SLOT, PASS):
        rows = min(PASS, SLOT - first)
        index = lax.broadcasted_iota(jnp.int32, (rows, lanes), 1) // group
        v = [read(n, slice(first, first + rows)) for n in range(count)]
        k = count // 2
        while k:
            low_part = (index & k) == 0
            pairs = [(i, i | k) for i in range(count) if not i & k]
            moved = [
                (pltpu.roll(v[j], k * group, 1), pltpu.roll(v[i], lanes - k * group, 1))
                for i, j in pairs
            ]
            for (i, j), (from_j, from_i) in zip(pairs, moved, strict=True):
                v[i] = jnp.where(low_part, v[i], from_j)
                v[j] = jnp.where(low_part, from_i, v[j])
            k //= 2
        start = BASE - SHIFT + first
        for i in planes:
            write(i, slice(start, start + rows), v[i])


def one_sided(pm2, pm1, p0, pp1, pp2, positive):
    p1 = jnp.where(positive, pm2, pp2)
    p2 = jnp.where(positive, pm1, pp1)
    p4 = jnp.where(positive, pp1, pm1)
    r2 = p0 - p2
    t1 = r2 - (p2 - p1)
    t2 = (p4 - p0) - r2
    k = 39.0 / 64.0
    eps = 0.75 * weno_eps
    c2 = (k * p2) * p2 + eps
    c0 = (k * p0) * p0 + eps
    y1 = p1 - 1.375 * p2
    y2 = p0 - 0.625 * p2
    y3 = p4 - 1.375 * p0
    s1 = y1 * y1 + c2
    s2 = y2 * y2 + c2
    s3 = y3 * y3 + c0
    g1, g2, g3 = [over * over for over in (1.0 / s1, 1.0 / s2, 1.0 / s3)]
    g3 = 3.0 * g3
    return r2 + (g1 * (t1 + t1) + g3 * t2) / ((g1 + g3) + 6.0 * g2)


def stage(src, base, dst, coef_refs, scale_ref, lo, count, parts, rows=None):
    keep, mix = parts
    lanes = src.shape[2]

    def along_lanes(f):
        lane = lax.broadcasted_iota(jnp.int32, f.shape, 1)
        fp = jnp.where(lane == lanes - 1, f, pltpu.roll(f, lanes - 1, 1))
        fm = jnp.where(lane == 0, f, pltpu.roll(f, 1, 1))
        return (fp - f) - (f - fm), fp - fm

    for start, step_rows in rows or [(n, STEP) for n in range(FIRST, FIRST + SPAN, STEP)]:
        part = slice(start, start + step_rows)
        coefs = [ref[part, :] for ref in coef_refs]
        lane = lax.broadcasted_iota(jnp.int32, (step_rows, lanes), 1)

        def at(x, shift=0, start=start, step_rows=step_rows):
            return src[x, start + shift : start + shift + step_rows, :]

        def body(i, carry, part=part, coefs=coefs, lane=lane, at=at):
            x = lo + i
            pm2, pm1, p0, pp1, last, q0, across = carry
            f = at(x)
            following = along_lanes(at(x + 1))
            qm1 = jnp.where(lane < 1, 0.0, pltpu.roll(q0, 1, 1))
            qm2 = jnp.where(lane < 2, 0.0, pltpu.roll(q0, 2, 1))
            qp1 = jnp.where(lane > lanes - 2, 0.0, pltpu.roll(q0, lanes - 1, 1))
            qp2 = jnp.where(lane > lanes - 3, 0.0, pltpu.roll(q0, lanes - 2, 1))
            ahead, near = at(x + 3), at(x + 2)
            step = ahead - near
            pp2 = step - last
            speed = scale_ref[0, x] * coefs[0]
            total = speed * (at(x + 1) - at(x - 1))
            damp = jnp.abs(speed) * one_sided(pm2, pm1, p0, pp1, pp2, speed > 0)
            z = [at(x, shift) for shift in (-3, -2, -1)] + [f]
            z = z + [at(x, shift) for shift in (1, 2, 3)]
            d = [z[n + 1] - z[n] for n in range(6)]
            q = [d[n + 1] - d[n] for n in range(5)]
            speed = scale_ref[2, x] * coefs[2]
            total = total + speed * (z[4] - z[2])
            damp = damp + jnp.abs(speed) * one_sided(*q, speed > 0)
            speed = scale_ref[1, x] * coefs[1]
            total = total + speed * across
            damp = damp + jnp.abs(speed) * one_sided(qm2, qm1, q0, qp1, qp2, speed > 0)
            moved = f - (total - (1.0 / 3.0) * damp)
            if base is not None:
                moved = keep * base[x, part, :] + mix * moved
            dst[x, part, :] = moved
            return (pm1, p0, pp1, pp2, step, *following)

        f = [at(lo + n) for n in range(-3, 3)]
        d = [f[n + 1] - f[n] for n in range(5)]
        p = [d[n + 1] - d[n] for n in range(4)]
        lax.fori_loop(0, count, body, (p[0], p[1], p[2], p[3], d[4], *along_lanes(at(lo))))


def clamp_planes(ref, first, last, lo, hi, begin, end):
    @pl.when(first)
    def _():
        def fill(i, carry):
            ref[lo + i] = ref[begin]
            return carry

        lax.fori_loop(0, begin - lo, fill, 0)

    @pl.when(last)
    def _():
        def fill(i, carry):
            ref[end + i] = ref[end - 1]
            return carry

        lax.fori_loop(0, hi - end, fill, 0)


def clamp_rows(ref, first, last, lo, hi, depth):
    @pl.when(first)
    def _():
        def fill(i, carry):
            x = lo + i
            ref[x, FIRST:BASE, :] = jnp.broadcast_to(
                ref[x, BASE : BASE + 1, :], (BASE - FIRST, ref.shape[2])
            )
            return carry

        lax.fori_loop(0, hi - lo, fill, 0)

    @pl.when(last)
    def _():
        def fill(i, carry):
            x = lo + i
            top = BASE + depth
            ref[x, top : FIRST + SPAN, :] = jnp.broadcast_to(
                ref[x, top - 1 : top, :], (FIRST + SPAN - top, ref.shape[2])
            )
            return carry

        lax.fori_loop(0, hi - lo, fill, 0)


def one_side(positive, s, behind, ahead):
    drop = s - jnp.minimum(behind, ahead)
    rise = jnp.maximum(behind, ahead) - s
    steep = jnp.maximum(jnp.where(positive, drop, rise), 0.0)
    return steep * steep


def sweep(src, dst, lo, count):
    lanes = src.shape[2]

    def body(i, carry):
        x = lo + i
        for start, step_rows in LATE:
            start = start + 1
            lane = lax.broadcasted_iota(jnp.int32, (step_rows, lanes), 1)

            def at(x, shift=0, start=start, step_rows=step_rows):
                return src[x, start + shift : start + shift + step_rows, :]

            s = at(x)
            positive = s > 0
            sp = jnp.where(lane == lanes - 1, s, pltpu.roll(s, lanes - 1, 1))
            sm = jnp.where(lane == 0, s, pltpu.roll(s, 1, 1))
            total = one_side(positive, s, at(x - 1), at(x + 1))
            total = total + one_side(positive, s, at(x, -1), at(x, 1))
            total = total + one_side(positive, s, sm, sp)
            total = total + gradient_eps
            size = total * lax.rsqrt(total)
            sign = s * lax.rsqrt(s * s + 1.0)
            dst[x, start : start + step_rows, :] = s - pseudo_step * sign * (size - 1.0)
        return carry

    lax.fori_loop(0, count, body, 0)


def ends(place_ref):
    first_x = place_ref[0] == 0
    last_x = place_ref[0] == place_ref[2] - 1
    first_z = place_ref[1] == 0
    last_z = place_ref[1] == place_ref[3] - 1
    return first_x, last_x, first_z, last_z


def inner_kernel(place_ref, scale_ref, u_ref, v_ref, w_ref, slots_ref, f0, f1, f2):
    count, halves, _, lanes = slots_ref.shape
    own = halves * count
    _, _, first_z, last_z = ends(place_ref)
    for h in range(halves):

        def write(i, rows, value, h=h):
            f0[EDGE + h * count + i, rows, :] = value

        regroup(lambda n, at, h=h: slots_ref[n, h, at, :], count, lanes, range(count), write)
    coefs = (u_ref, v_ref, w_ref)
    stage(f0, None, f1, coefs, scale_ref, EDGE + 3, own - 6, (0.0, 1.0))
    clamp_rows(f1, first_z, last_z, EDGE + 3, EDGE + own - 3, lanes)
    stage(f1, f0, f2, coefs, scale_ref, EDGE + 6, own - 12, (0.75, 0.25))
    clamp_rows(f2, first_z, last_z, EDGE + 6, EDGE + own - 6, lanes)


def outer_kernel(
    place_ref, scale_ref, u_ref, v_ref, w_ref, below_ref, above_ref, f0_in, f1_in, f2_in,
    f0, f1, f2, up_ref, down_ref,
):
    del f0_in, f1_in, f2_in
    count, _, lanes = below_ref.shape
    begin, end = EDGE, f0.shape[0] - EDGE
    first_x, last_x, first_z, last_z = ends(place_ref)
    for ref, at_plane, planes in (
        (below_ref, begin - count, range(count - 6, count)),
        (above_ref, end, range(6)),
    ):

        def write(i, rows, value, at_plane=at_plane):
            f0[at_plane + i, rows, :] = value

        regroup(lambda n, at, ref=ref: ref[n, at, :], count, lanes, planes, write)
    clamp_planes(f0, first_x, last_x, begin - 6, end + 6, begin, end)
    coefs = (u_ref, v_ref, w_ref)
    for lo, hi in ((begin - 3, begin + 3), (end - 3, end + 3)):
        stage(f0, None, f1, coefs, scale_ref, lo, hi - lo, (0.0, 1.0))
    clamp_planes(f1, first_x, last_x, begin - 3, end + 3, begin, end)
    for lo, hi in ((begin - 3, begin + 3), (end - 3, end + 3)):
        clamp_rows(f1, first_z, last_z, lo, hi, lanes)
    for lo, hi in ((begin, begin + HIGH), (end - LOW, end)):
        stage(f1, f0, f2, coefs, scale_ref, lo, hi - lo, (0.75, 0.25))
        clamp_rows(f2, first_z, last_z, lo, hi, lanes)
    for ref, start in ((up_ref, end - LOW), (down_ref, begin)):
        for i in range(ref.shape[0]):
            ref[i] = f2[start + i]


def third_kernel(place_ref, scale_ref, u_ref, v_ref, w_ref, f0, f1, f2_in, f2, f3):
    del f2_in
    _, _, first_z, last_z = ends(place_ref)
    begin, end = EDGE, f0.shape[0] - EDGE
    coefs = (u_ref, v_ref, w_ref)
    for lo, hi in ((begin + HIGH, begin + 6), (end - 6, end - LOW)):
        stage(f1, f0, f2, coefs, scale_ref, lo, hi - lo, (0.75, 0.25))
        clamp_rows(f2, first_z, last_z, lo, hi, f2.shape[2])
    lo, hi = begin + 3, end - 3
    stage(f2, f0, f3, coefs, scale_ref, lo, hi - lo, (1.0 / 3.0, 2.0 / 3.0), LATE)


def last_kernel(
    place_ref, scale_ref, u_ref, v_ref, w_ref, below_ref, above_ref, f0, f2_in, f3_in,
    f2, f3, slots_ref, lower_ref, upper_ref, f4,
):
    del f2_in, f3_in
    begin, end = EDGE, f0.shape[0] - EDGE
    own, depth = end - begin, lower_ref.shape[2]
    first_x, last_x, first_z, last_z = ends(place_ref)
    for ref, start in ((below_ref, begin - LOW), (above_ref, end)):
        for i in range(ref.shape[0]):
            f2[start + i] = ref[i]
    clamp_planes(f2, first_x, last_x, begin - LOW, end + HIGH, begin, end)
    coefs = (u_ref, v_ref, w_ref)
    for lo, hi in ((begin - 1, begin + 3), (end - 3, end + 2)):
        stage(f2, f0, f3, coefs, scale_ref, lo, hi - lo, (1.0 / 3.0, 2.0 / 3.0), LATE)
    clamp_planes(f3, first_x, last_x, begin - 1, end + 2, begin, end)
    clamp_rows(f3, first_z, last_z, begin - 1, end + 2, depth)
    sweep(f3, f4, begin, own + 1)
    clamp_planes(f4, jnp.bool_(False), last_x, begin, end + 1, begin, end)
    clamp_rows(f4, jnp.bool_(False), last_z, begin, end + 1, depth)
    count = slots_ref.shape[0]
    piece = depth // count

    def turn(i, carry):
        lower = f4[begin + i, BASE : BASE + depth, :].T
        upper = f4[begin + i, BASE + 1 : BASE + 1 + depth, :].T
        for ref, value in ((lower_ref, lower), (upper_ref, upper)):
            ref[i, 0:depth, :] = value
            ref[i, depth : depth + 8, :] = jnp.broadcast_to(value[depth - 1 : depth], (8, depth))

        @pl.when(i < own)
        def _():
            for d in range(count):
                slots_ref[d, i] = lower[d * piece : (d + 1) * piece]

        return carry

    lax.fori_loop(0, own + 1, turn, 0)


def store_edge(refs, at, a, b):
    weight = 1.0 / (1.0 + jnp.exp2((sharpness * 1.4426950408889634) * (a * b)))
    low = a * a + crossing_bias
    part = low / (low + (b * b + crossing_bias))
    along = b - a
    scaled = weight * along
    for ref, value in zip(
        refs, (weight, part, scaled, scaled * along, weight * part, part * along), strict=True
    ):
        ref[at] = value


def add(old, new):
    return new if old is None else old + new


def contour_kernel(lower_ref, upper_ref, out_ref, *scratch):
    planes, _, lanes = lower_ref.shape
    depth = lanes
    sides = (lower_ref, upper_ref)
    x_edges, y_edges, z_edges = scratch[0:6], scratch[6:12], scratch[12:18]

    def across_edges(x, carry):
        for start in range(0, depth + 8, 8):
            at = slice(start, start + 8)
            store_edge(z_edges, (x, at), lower_ref[x, at, :], upper_ref[x, at, :])
            if start < depth:
                for n, ref in enumerate(sides):
                    there = ref[x, start + 1 : start + 9, :]
                    store_edge(y_edges, (n, x, at), ref[x, at, :], there)
        return carry

    @pl.when(pl.program_id(0) == 0)
    def _():
        lax.fori_loop(0, planes, across_edges, 0)

    def cubes(x):
        for start in range(0, depth + 8, 8):
            at = slice(start, start + 8)
            for n, ref in enumerate(sides):
                store_edge(x_edges, (n, at), ref[x, at, :], ref[x + 1, at, :])
        for start in range(0, depth, 8):

            def rows(bit, start=start):
                return slice(start + bit, start + bit + 8)

            f = {}
            for bx in (0, 1):
                for by in (0, 1):
                    for bz in (0, 1):
                        f[bx, by, bz] = sides[bz][x + bx, rows(by), :]
            diff = {}
            for d in range(3):
                for key in sorted(f):
                    if key[d] == 0:
                        diff[d, key] = f[set_bit(key, d, 1)] - f[key]
            total = None
            mass = [None] * 3
            moment = {}
            target = [None] * 3
            twist = {}
            for d in range(3):
                a1, a2 = [a for a in range(3) if a != d]
                weights = {}
                for key in sorted(f):
                    if key[d] != 0:
                        continue
                    bx, by, bz = key
                    refs, at = (
                        (x_edges, (bz, rows(by))),
                        (y_edges, (bz, x + bx, rows(0))),
                        (z_edges, (x + bx, rows(by))),
                    )[d]
                    weight, part, scaled_d, square, moved, height = [ref[at] for ref in refs]
                    weights[key[a1], key[a2]] = weight
                    mass[d] = add(mass[d], moved)
                    normal = [None] * 3
                    normal[d] = diff[d, key]
                    scaled = [None] * 3
                    scaled[d] = scaled_d
                    projection = height
                    for a in (a1, a2):
                        low = diff[a, set_bit(key, a, 0)]
                        third = 3 - a - d
                        name = (third, key[third])
                        if name not in twist:
                            twist[name] = diff[a, set_bit(set_bit(key, a, 0), d, 1)] - low
                        normal[a] = low + part * twist[name]
                        scaled[a] = weight * normal[a]
                        if key[a] == 1:
                            projection = projection + normal[a]
                    for i in range(3):
                        for j in range(i, 3):
                            if i == d and j == d:
                                value = square
                            elif j == d:
                                value = scaled[j] * normal[i]
                            else:
                                value = scaled[i] * normal[j]
                            moment[i, j] = add(moment.get((i, j)), value)
                        target[i] = add(target[i], scaled[i] * projection)
                ends = weights[1, 0] + weights[1, 1]
                mass[a1] = add(mass[a1], ends)
                mass[a2] = add(mass[a2], weights[0, 1] + weights[1, 1])
                total = add(total, (weights[0, 0] + weights[0, 1]) + ends)
            inverse = tikhonov / (total + mass_prior)
            r0, r1, r2 = [target[i] + (mass[i] + 0.5 * mass_prior) * inverse for i in range(3)]
            over0 = 1.0 / (moment[0, 0] + tikhonov)
            l1 = moment[0, 1] * over0
            l2 = moment[0, 2] * over0
            over1 = 1.0 / ((moment[1, 1] + tikhonov) - l1 * moment[0, 1])
            rest = moment[1, 2] - l1 * moment[0, 2]
            l3 = rest * over1
            over2 = 1.0 / (((moment[2, 2] + tikhonov) - l2 * moment[0, 2]) - l3 * rest)
            r1 = r1 - l1 * r0
            r2 = (r2 - l2 * r0) - l3 * r1
            x2 = r2 * over2
            x1 = r1 * over1 - l3 * x2
            out_ref[0, 0, rows(0), :] = (r0 * over0 - l1 * x1) - l2 * x2
            out_ref[1, 0, rows(0), :] = x1
            out_ref[2, 0, rows(0), :] = x2

    cubes(pl.program_id(0))


def set_bit(key, d, value):
    listed = list(key)
    listed[d] = value
    return tuple(listed)


def speeds(flow_amplitude, x_start, z_start, own, depth, total_x, total_y, total_z):
    def cells(start, count, total):
        return ((start + jnp.arange(count, dtype=jnp.int32)).astype(jnp.float32) + 0.5) / total

    x = cells(x_start - EDGE, EDGE + own + EDGE, total_x)
    y = cells(0, total_y, total_y)
    z = cells(z_start - BASE, ROWS, total_z)
    half_x, full_x = jnp.sin(jnp.pi * x) ** 2, jnp.sin(2.0 * jnp.pi * x)
    half_y, full_y = jnp.sin(jnp.pi * y) ** 2, jnp.sin(2.0 * jnp.pi * y)
    half_z, full_z = jnp.sin(jnp.pi * z) ** 2, jnp.sin(2.0 * jnp.pi * z)
    scale = jnp.stack(
        [
            flow_amplitude[0] * half_x,
            -0.5 * flow_amplitude[1] * full_x,
            -0.5 * flow_amplitude[2] * full_x,
        ]
    )
    u = full_z[:, None] * full_y[None, :]
    v = full_z[:, None] * half_y[None, :]
    w = half_z[:, None] * full_y[None, :]
    return scale, u, v, w


def near(value):
    return pltpu.with_memory_space_constraint(value, pltpu.VMEM)


def shards(level_set, flow_amplitude):
    own, cols, layers = level_set.shape
    count_x, count_z = lax.axis_size("px"), lax.axis_size("py")
    at_x, at_z = lax.axis_index("px"), lax.axis_index("py")
    depth, wide = layers // count_z, cols * count_z
    lanes = 128
    halves = own * cols // lanes
    f32 = jnp.float32
    slots = pl.pallas_call(
        pack_kernel,
        out_shape=pltpu.VMEM((count_z, halves, SLOT, lanes), f32),
        in_specs=[VMEM],
        out_specs=VMEM,
        scratch_shapes=[pltpu.VMEM((halves, layers + 32, lanes), f32)],
        compiler_params=PARAMS,
        name="pack",
    )(level_set.reshape(own * cols, layers))
    slots = lax.all_to_all(slots, "py", split_axis=0, concat_axis=0, tiled=True)
    scale, u, v, w = speeds(
        flow_amplitude, at_x * own, at_z * depth, own, depth, own * count_x, wide, layers
    )
    place = jnp.stack([at_x, at_z, jnp.int32(count_x), jnp.int32(count_z)]).astype(jnp.int32)
    ring = [(i, (i + 1) % count_x) for i in range(count_x)]
    back_ring = [(b, a) for a, b in ring]
    below = lax.ppermute(slots[:, halves - 1], "px", ring)
    above = lax.ppermute(slots[:, 0], "px", back_ring)
    planes = EDGE + own + EDGE
    field = pltpu.VMEM((planes, ROWS, wide), f32)
    coefs = [near(a) for a in (u, v, w)]
    f0, f1, f2 = pl.pallas_call(
        inner_kernel,
        out_shape=[field] * 3,
        in_specs=[SMEM, SMEM] + [VMEM] * 4,
        out_specs=[VMEM] * 3,
        compiler_params=PARAMS,
        name="inner",
    )(place, scale, *coefs, near(slots))
    f0, f1, f2, up, down = pl.pallas_call(
        outer_kernel,
        out_shape=[field, field, field]
        + [pltpu.VMEM((n, ROWS, wide), f32) for n in (LOW, HIGH)],
        in_specs=[SMEM, SMEM] + [VMEM] * 8,
        out_specs=[VMEM] * 5,
        input_output_aliases={7: 0, 8: 1, 9: 2},
        compiler_params=PARAMS,
        name="outer",
    )(place, scale, *coefs, near(below), near(above), near(f0), near(f1), near(f2))
    below = lax.ppermute(up, "px", ring)
    above = lax.ppermute(down, "px", back_ring)
    f2, f3 = pl.pallas_call(
        third_kernel,
        out_shape=[field, field],
        in_specs=[SMEM, SMEM] + [VMEM] * 6,
        out_specs=[VMEM] * 2,
        input_output_aliases={7: 0},
        compiler_params=PARAMS,
        name="third",
    )(place, scale, *coefs, near(f0), near(f1), near(f2))
    _, _, turned, lower, upper = pl.pallas_call(
        last_kernel,
        out_shape=[
            field,
            field,
            pltpu.VMEM((count_z, own, cols, depth), f32),
            pltpu.VMEM((own + 1, wide + 8, depth), f32),
            pltpu.VMEM((own + 1, wide + 8, depth), f32),
        ],
        in_specs=[SMEM, SMEM] + [VMEM] * 8,
        out_specs=[VMEM] * 5,
        scratch_shapes=[field],
        input_output_aliases={8: 0, 9: 1},
        compiler_params=PARAMS,
        name="last",
    )(place, scale, *coefs, near(below), near(above), near(f0), near(f2), near(f3))
    back = lax.all_to_all(turned, "py", split_axis=0, concat_axis=0, tiled=True)
    phi_next = jnp.moveaxis(back, 0, 2).reshape(own, cols, layers)
    vertices = pl.pallas_call(
        contour_kernel,
        out_shape=jax.ShapeDtypeStruct((3, own, wide, depth), f32),
        grid=(own,),
        in_specs=[VMEM] * 2,
        out_specs=pl.BlockSpec((3, 1, wide, depth), lambda i: (0, i, 0, 0)),
        scratch_shapes=[pltpu.VMEM((2, wide + 8, depth), f32)] * 6
        + [pltpu.VMEM((2, own + 1, wide, depth), f32)] * 6
        + [pltpu.VMEM((own + 1, wide + 8, depth), f32)] * 6,
        compiler_params=WIDE_PARAMS,
        name="contour",
    )(near(lower), near(upper))
    return (phi_next, vertices)


def solution(mesh):
    in_specs = (P("px", "py", None), P())
    out_specs = (P("px", "py", None), P(None, "px", None, "py"))
    return jax.shard_map(shards, mesh=mesh, in_specs=in_specs, out_specs=out_specs, check_vma=False)
```
